32 devices in a mesh: groups: 2 (over x), ctx: 16 (over z, y, core).
Axes of the slice: x: 2, y: 2, z: 4, core: 2. Of those that a mesh axis runs over, the one named last changes fastest.
Arguments:
- queries: bfloat16 [512, 4096], P(('groups', 'ctx')), parts along dimension 0, may hold values from -12 to 12
- new_key: bfloat16 [512, 512], P(('groups', 'ctx')), parts along dimension 0, may hold values from -8 to 8
- new_value: bfloat16 [512, 512], P(('groups', 'ctx')), parts along dimension 0, may hold values from -6 to 6
- key_cache: bfloat16 [32768, 512], P(('groups', 'ctx')), parts along dimension 0, may hold values from -8 to 8
- value_cache: bfloat16 [32768, 512], P(('groups', 'ctx')), parts along dimension 0, may hold values from -6 to 6
- cache_len: int32 [512], P('groups'), parts along dimension 0, may hold values from 1 to 16384
- out_weight: bfloat16 [4096, 2048], P('ctx'), may hold values from -0.09375 to 0.09375
- residual: bfloat16 [512, 2048], P(('groups', 'ctx')), parts along dimension 0, may hold values from -8 to 8
- norm_gain: bfloat16 [2048], replicated, may hold values from 0.099609375 to 1.8984375
- expert_ids: int32 [512, 8], P(('groups', 'ctx')), parts along dimension 0, may hold values from 0 to 31, all different within a row; in each aligned block of 16 rows (0 to 15, 16 to 31, ...) at most 4 rows name the same one
- route_weight: float32 [512, 8], P(('groups', 'ctx')), parts along dimension 0, may hold values from 0.1 to 1
- w_gate: bfloat16 [32, 2048, 768], P('ctx'), may hold values from -0.125 to 0.125
- w_up: bfloat16 [32, 2048, 768], P('ctx'), may hold values from -0.125 to 0.125
- w_down: bfloat16 [32, 768, 2048], P('ctx'), may hold values from -0.21875 to 0.21875
Outputs:
- layer_out: bfloat16 [512, 2048], P(('groups', 'ctx')), parts along dimension 0
The draws below stay inside these ranges and needn't reach their ends.
There are 2 independent parts, one for each index of `groups`. The reference program is written for one: setup_inputs(seed, part) draws one part's arguments, and reference() takes and returns one part's arrays. A program takes and returns all parts, laid end to end along the dimension named above; an argument that names none is the same for every part. Nothing has to cross between parts.
Inputs may be any that keep to these rules, and one draw needn't show every extreme that they name: `expert_ids`: among the rows of one device no expert is named more than 4 times.
All inputs are finite; a program needn't handle non-finite values.
Results may differ from the reference program's by a relative error of at most 0.018.
Values may be sent and summed in bfloat16 or wider, within the bound.
A program may use at most 192 MiB of HBM per device.

```python
import math
import jax
import jax.numpy as jnp
import numpy as np
from jax import lax

D = 2048
HEADS = 32
KVH = 4
HD = 128
FF = 768
TOP = 8
ROWS_DEV = 16
EXPERTS = 32
ROWS = 256
CTX = 16384
MOST = 4


def draw_queries(key, part):
    own_key = jax.random.fold_in(key, 11)
    values = jnp.clip(2.0 * jax.random.normal(own_key, (ROWS, HEADS * HD)), -8.0, 8.0)
    return values.astype(jnp.bfloat16)


def draw_key_cache(key, part):
    own_key = jax.random.fold_in(key, 12)
    values = jnp.clip(1.5 * jax.random.normal(own_key, (CTX, KVH * HD)), -8.0, 8.0)
    return values.astype(jnp.bfloat16)


def draw_new_key(key, part):
    own_key = jax.random.fold_in(key, 13)
    values = jnp.clip(2.5 * jax.random.normal(own_key, (ROWS, KVH * HD)), -8.0, 8.0)
    return values.astype(jnp.bfloat16)


def draw_residual(key, part):
    own_key = jax.random.fold_in(key, 14)
    noise_key = jax.random.fold_in(own_key, 0)
    values = jax.random.normal(noise_key, (ROWS, D))
    values = jnp.clip(values, -6.0, 6.0)
    return values.astype(jnp.bfloat16)


def with_ends(drawn, stream_key, least, top_value):
    dims = drawn.shape
    spot = [jax.random.randint(jax.random.fold_in(stream_key, axis), (), 0, dims[axis]) for axis in range(len(dims))]
    drawn = drawn.at[tuple(spot)].set(least)
    longest = dims.index(max(dims))
    spot[longest] = (spot[longest] + 1) % dims[longest]
    return drawn.at[tuple(spot)].set(top_value)


def block_levels(stream_key, dims, cuts, least, top_value):
    level = 1.0
    for dim, parts in cuts:
        steps = jax.random.uniform(jax.random.fold_in(jax.random.fold_in(stream_key, 6), dim), (parts,), jnp.float32, least / len(cuts), top_value / len(cuts))
        level = level * jnp.repeat(jnp.exp(steps), dims[dim] // parts).reshape((-1,) + (1,) * (len(dims) - 1 - dim))
    return level


def routed_block(key, own, number, rows, count, top, reach, lean):
    order = jax.random.permutation(key, count)
    packed, ordinary = load_shares(count, rows * top, reach, lean, True), load_shares(count, rows * top, reach, lean, False)
    places = jnp.arange(count)

    def named(sizes, turn):
        used = int((sizes > 0).sum())
        fixed = max(1, used // 4)
        moved = fixed + (places - fixed + turn * (used - fixed)) % max(1, count - fixed)
        return jnp.zeros((count,), jnp.int32).at[order[jnp.where(places < fixed, places, moved)]].set(jnp.asarray(sizes, jnp.int32))

    sizes = jnp.where(number % 4 == 0, named(packed, number // 4), named(ordinary, number - number // 4 - 1))
    mixed = jax.random.permutation(jax.random.fold_in(own, 3), count)
    donor, taker = mixed[0:count // 2 * 2:2], mixed[1:count // 2 * 2:2]
    slack = jnp.minimum(sizes[donor] - 1, reach - sizes[taker]) // 2
    slack = jnp.where((donor == order[0]) | (taker == order[0]) | (sizes[taker] == 0), 0, jnp.maximum(slack, 0))
    moved = jax.random.randint(jax.random.fold_in(own, 4), (count // 2,), 0, 1 << 20) % (slack + 1)
    sizes = sizes.at[donor].add(-moved).at[taker].add(moved)
    labels = jnp.searchsorted(jnp.cumsum(sizes), jnp.arange(rows * top), side="right").astype(jnp.int32)
    table = labels.reshape(top, rows).T
    table = table[jax.random.permutation(jax.random.fold_in(own, 1), rows)]
    turn = jax.random.randint(jax.random.fold_in(own, 2), (rows, 1), 0, top)
    return jnp.take_along_axis(table, (jnp.arange(top)[None, :] + turn) % top, axis=1)


def load_shares(amount, total, limit, skew, full):
    loads = [(1 << 20) // math.isqrt(rank ** skew) + 1 for rank in range(1, amount + 1)]
    largest = limit if full else min(limit, max(-(-total // amount), total * loads[0] // sum(loads)))
    least = 1 if total - largest >= amount - 1 else 0
    holding, spare = [largest] + [least] * (amount - 1), total - largest - least * (amount - 1)
    while spare > 0:
        free = [i for i in range(1, amount) if holding[i] < largest] or [i for i in range(1, amount) if holding[i] < limit]
        mass, left = sum([loads[i] for i in free]), spare
        for i in free:
            addition = min(limit - holding[i], max(1, left * loads[i] // mass), spare)
            holding[i] = holding[i] + addition
            spare = spare - addition
    return np.array(holding)


def centred(stream_key, extent, scale, limit, cuts=(), kind=jnp.bfloat16):
    entries = jax.random.normal(stream_key, extent, jnp.float32) * scale
    if len(cuts) > 0:
        entries = block_levels(stream_key, extent, cuts, -0.22, 0.18) * entries
    return jnp.clip(entries, min=-limit, max=limit).astype(kind)


def setup_inputs(seed: int = 0, part: int = 0) -> dict:
    splits = jax.random.split(jax.random.key(seed), 15)
    part_splits = jax.random.split(jax.random.fold_in(splits[14], part), 15)
    queries = draw_queries(jax.random.fold_in(jax.random.fold_in(splits[14], part), 71), part)
    new_key = draw_new_key(jax.random.fold_in(jax.random.fold_in(splits[14], part), 71), part)
    new_value = centred(part_splits[2], (ROWS, KVH * HD), 1.0, 6.0, ((0, 16),))
    key_cache = draw_key_cache(jax.random.fold_in(jax.random.fold_in(splits[14], part), 71), part)
    value_cache = centred(part_splits[4], (CTX, KVH * HD), 1.0, 6.0, ((0, 16),))
    cache_len = with_ends(jax.random.randint(part_splits[5], (ROWS,), 1, CTX + 1), jax.random.fold_in(part_splits[5], 1), 1, CTX).astype(jnp.int32)
    out_weight = centred(splits[6], (HEADS * HD, D), (HEADS * HD) ** -0.5, 0.09375, ((0, 16),))
    residual = draw_residual(jax.random.fold_in(jax.random.fold_in(splits[14], part), 71), part)
    norm_gain = jnp.clip(1.0 + 0.18 * jax.random.normal(splits[8], (D,), jnp.float32), 0.099609375, 1.8984375).astype(jnp.bfloat16)
    expert_ids_keys = jax.random.split(jax.random.fold_in(part_splits[9], 1), ROWS // ROWS_DEV)
    expert_ids_turns = jax.random.permutation(jax.random.fold_in(part_splits[9], 3), ROWS // ROWS_DEV)
    expert_ids = jax.vmap(lambda own, number: routed_block(jax.random.fold_in(part_splits[9], 2), own, number, ROWS_DEV, EXPERTS, TOP, MOST, 2))(expert_ids_keys, expert_ids_turns).reshape((ROWS, TOP))
    route_weight = jnp.clip(jnp.exp(math.log(1.0) - 2.3025851 * jax.random.uniform(part_splits[10], (ROWS, TOP), jnp.float32) ** block_levels(part_splits[10], (ROWS, TOP), ((0, 16),), -0.2, 0.2)), 0.1, 1.0)
    w_gate = centred(splits[11], (EXPERTS, D, FF), D ** -0.5, 0.125, ((0, 16),))
    w_up = centred(splits[12], (EXPERTS, D, FF), D ** -0.5, 0.125, ((0, 16),))
    w_down = centred(splits[13], (EXPERTS, FF, D), FF ** -0.5, 0.21875, ((0, 16),))
    return {"queries": queries, "new_key": new_key, "new_value": new_value, "key_cache": key_cache, "value_cache": value_cache, "cache_len": cache_len, "out_weight": out_weight, "residual": residual, "norm_gain": norm_gain, "expert_ids": expert_ids, "route_weight": route_weight, "w_gate": w_gate, "w_up": w_up, "w_down": w_down}


def reference(queries, new_key, new_value, key_cache, value_cache, cache_len, out_weight, residual, norm_gain, expert_ids, route_weight, w_gate, w_up, w_down):
    total_rows = queries.shape[0]
    cache_total = key_cache.shape[0]
    group_size = HEADS // KVH
    score_scale = 1.0 / math.sqrt(HD)
    query_heads = queries.astype(jnp.float32).reshape(total_rows, KVH, group_size, HD)
    fresh_keys = new_key.astype(jnp.float32).reshape(total_rows, KVH, HD)
    fresh_values = new_value.astype(jnp.float32).reshape(total_rows, KVH, HD)
    cached_keys = key_cache.astype(jnp.float32).reshape(cache_total, KVH, HD)
    cached_values = value_cache.astype(jnp.float32).reshape(cache_total, KVH, HD)
    fresh_scores = jnp.einsum('rgqd,rgd->rgq', query_heads, fresh_keys) * score_scale
    block_rows = 16

    def attend(block_index):
        first_row = (block_index * block_rows).astype(jnp.int32)
        query_block = lax.dynamic_slice_in_dim(query_heads, first_row, block_rows, 0)
        fresh_block = lax.dynamic_slice_in_dim(fresh_scores, first_row, block_rows, 0)
        value_block = lax.dynamic_slice_in_dim(fresh_values, first_row, block_rows, 0)
        length_block = lax.dynamic_slice_in_dim(cache_len, first_row, block_rows, 0)
        scores = jnp.einsum('rgqd,pgd->rgqp', query_block, cached_keys) * score_scale
        visible = jnp.arange(cache_total, dtype=jnp.int32)[None, :] < length_block[:, None]
        scores = jnp.where(visible[:, None, None, :], scores, -jnp.inf)
        row_peak = jnp.maximum(fresh_block, lax.optimization_barrier(jnp.max(scores, axis=-1)))
        weights = lax.optimization_barrier(jnp.exp(scores - row_peak[..., None]).astype(jnp.bfloat16)).astype(jnp.float32)
        numerator = jnp.einsum('rgqp,pgd->rgqd', weights, cached_values)
        denominator = lax.optimization_barrier(jnp.sum(weights, axis=-1))
        fresh_weight = lax.optimization_barrier(jnp.exp(fresh_block - row_peak).astype(jnp.bfloat16)).astype(jnp.float32)
        numerator = numerator + fresh_weight[..., None] * value_block[:, :, None, :]
        denominator = denominator + fresh_weight
        return (numerator / denominator[..., None]).astype(jnp.bfloat16).reshape(block_rows, HEADS * HD)
    attended = lax.map(attend, jnp.arange(total_rows // block_rows, dtype=jnp.int32)).reshape(total_rows, HEADS * HD)
    attn_out = jnp.dot(attended, out_weight, preferred_element_type=jnp.float32)
    after_attention = lax.optimization_barrier((residual.astype(jnp.float32) + attn_out).astype(jnp.bfloat16))
    middle = after_attention.astype(jnp.float32)
    inv_rms = lax.rsqrt(lax.optimization_barrier(jnp.mean(middle * middle, axis=-1, keepdims=True)) + 1e-06)
    normed = (middle * inv_rms * norm_gain.astype(jnp.float32)[None, :]).astype(jnp.bfloat16)
    expert_total = w_gate.shape[0]

    def add_expert(carry, inputs):
        gate_matrix, up_matrix, down_matrix, expert_number = inputs
        gate_proj = jnp.dot(normed, gate_matrix, preferred_element_type=jnp.float32)
        upward = jnp.dot(normed, up_matrix, preferred_element_type=jnp.float32)
        hidden = (jax.nn.silu(gate_proj) * upward).astype(jnp.bfloat16)
        produced = lax.optimization_barrier(jnp.dot(hidden, down_matrix, preferred_element_type=jnp.float32).astype(jnp.bfloat16))
        coefficient = lax.optimization_barrier(jnp.sum(jnp.where(expert_ids == expert_number, route_weight, 0.0), axis=1))
        return (carry + coefficient[:, None] * produced.astype(jnp.float32), None)
    mixed, _ = lax.scan(add_expert, jnp.zeros((total_rows, D), jnp.float32), (w_gate, w_up, w_down, jnp.arange(expert_total, dtype=jnp.int32)))
    return (middle + mixed).astype(jnp.bfloat16)
```

```python
import functools
import math

import jax
import jax.numpy as jnp
from jax import lax
from jax.experimental import pallas as pl
from jax.experimental.pallas import tpu as pltpu
from jax.sharding import PartitionSpec as P

HEADS = 32
KVH = 4
HD = 128
GROUP = HEADS // KVH
CORES = 2
NEG = -1e30
FLOOR = -1e29
MESH = pl.DeviceIdType.MESH
F32 = jnp.float32
BF16 = jnp.bfloat16
SCALE2 = math.log2(math.e) / math.sqrt(HD)


def remote(src, dst, send, recv, target):
    return pltpu.make_async_remote_copy(
        src_ref=src,
        dst_ref=dst,
        send_sem=send,
        recv_sem=recv,
        device_id={"ctx": target},
        device_id_type=MESH,
    )


def layer_kernel(
    n,
    ny,
    q_in,
    nv_in,
    fs_in,
    coef_in,
    kc_in,
    vc_in,
    len_ref,
    ow_in,
    res_ref,
    gain_ref,
    wg_in,
    wu_in,
    wd_in,
    out_ref,
    q_all,
    kc,
    vc,
    vt,
    coef,
    nvr,
    fsr,
    num,
    stat,
    rnum,
    rstat,
    ow,
    att,
    ost,
    r2,
    xn,
    wg,
    wu,
    wd,
    hid,
    acc,
    es,
    er,
    ost3,
    r3,
    aft,
    load_sem,
    kv_send,
    kv_recv,
    q_send,
    q_recv,
    q_relay_send,
    q_relay_recv,
    c_sems,
    f_send,
    f_recv,
    a_send,
    a_recv,
    b_send,
    b_recv,
    x_sems,
    e_sems,
    d_send,
    d_recv,
):
    chips = n // CORES
    nz = chips // ny
    half_chips = chips // CORES
    hpc = HEADS // chips
    rows = q_in.shape[0]
    all_rows = n * rows
    half_rows = chips * rows
    width = q_in.shape[1] // CORES
    kv_width = kc_in.shape[1] // CORES
    here = kc_in.shape[0]
    model = res_ref.shape[1]
    me = lax.axis_index("ctx")
    k = lax.rem(me, CORES)
    c = me // CORES
    z = c // ny
    y = lax.rem(c, ny)
    sister = c * CORES + 1 - k

    def chip_of(dz, dy):
        return lax.rem(z + dz, nz) * ny + lax.rem(y + dy, ny)

    loads = []

    def load(src, dst):
        copy = pltpu.make_async_copy(src, dst, load_sem.at[len(loads)])
        copy.start()
        loads.append(copy)
        return copy

    own_cols = pl.ds(pl.multiple_of(k * kv_width, 128), kv_width)
    other_cols = pl.ds(pl.multiple_of((1 - k) * kv_width, 128), kv_width)
    own_q = pl.ds(pl.multiple_of(k * width, 128), width)
    ld_k = load(kc_in.at[:, own_cols], kc.at[k])
    ld_v = load(vc_in.at[:, own_cols], vc.at[k])
    ld_q = load(q_in.at[:, own_q], q_all.at[k, c])
    ld_coef = load(coef_in, coef.at[k, c])
    kv_head = (c * hpc) // GROUP
    ld_nv = load(
        nv_in.at[:, pl.ds(pl.multiple_of(kv_head * HD, 128), HD)], nvr.at[c]
    )
    ld_fs = load(fs_in.at[c], fsr.at[c])
    ld_ow = load(ow_in, ow.at[k])

    barrier = pltpu.get_barrier_semaphore()
    for i in range(1, n):
        pl.semaphore_signal(
            barrier, inc=1, device_id={"ctx": lax.rem(me + i, n)}, device_id_type=MESH
        )
    pl.semaphore_wait(barrier, n - 1)

    pending = []

    q_first = {}
    for dz in range(nz):
        for dk in range(CORES):
            if dz == 0 and dk == 0:
                continue
            kt = lax.rem(k + dk, CORES)
            slot = dz * CORES + dk
            copy = remote(
                q_in.at[:, pl.ds(pl.multiple_of(kt * width, 128), width)],
                q_all.at[k, c],
                q_send.at[slot],
                q_recv.at[slot],
                chip_of(dz, 0) * CORES + kt,
            )
            copy.start()
            q_first[(dz, dk)] = copy
            pending.append(copy)
    q_second = []

    def relay_q(dz, dk, src):
        source_chip = chip_of(nz - dz, 0)
        source_core = lax.rem(k + dk, CORES)
        for dy in range(1, ny):
            slot = ((dy - 1) * nz + dz) * CORES + dk
            copy = remote(
                src,
                q_all.at[source_core, source_chip],
                q_relay_send.at[slot],
                q_relay_recv.at[slot],
                chip_of(0, dy) * CORES + k,
            )
            copy.start()
            q_second.append(copy)
            pending.append(copy)

    relay_q(0, 0, q_in.at[:, own_q])

    kv_copies = []
    for i, (src, dst) in enumerate(
        ((kc_in.at[:, other_cols], kc.at[k]), (vc_in.at[:, other_cols], vc.at[k]), (ow_in, ow.at[k]))
    ):
        copy = remote(src, dst, kv_send.at[i], kv_recv.at[i], sister)
        copy.start()
        kv_copies.append(copy)
        pending.append(copy)

    fresh_copies = []
    for j in range(1, chips):
        target = lax.rem(c + j, chips)
        cols = pl.ds(pl.multiple_of(((target * hpc) // GROUP) * HD, 128), HD)
        for i, (src, dst) in enumerate(((nv_in.at[:, cols], nvr.at[c]), (fs_in.at[target], fsr.at[c]))):
            copy = remote(src, dst, f_send.at[i, j], f_recv.at[i, j], target * CORES + k)
            copy.start()
            fresh_copies.append(copy)
            pending.append(copy)

    for src, dst in ((wg_in, wg), (wu_in, wu), (wd_in, wd)):
        load(src, dst)
    ld_w = loads[-3:]

    for dz in range(nz):
        for dk in range(CORES):
            if dz == 0 and dk == 0:
                continue
            q_first[(dz, dk)].wait_recv()
            relay_q(dz, dk, q_all.at[lax.rem(k + dk, CORES), chip_of(nz - dz, 0)])

    def gather(buf, sems):
        z_send, z_recv, y_send, y_recv, s_send, s_recv = sems
        lines = []
        for dz in range(1, nz):
            copy = remote(
                buf.at[k, c], buf.at[k, c], z_send.at[dz], z_recv.at[dz], chip_of(dz, 0) * CORES + k
            )
            copy.start()
            lines.append(copy)
            pending.append(copy)
        crossed, shared = [], []

        def cross(dz):
            source = chip_of(nz - dz, 0)
            for dy in range(1, ny):
                slot = dy * nz + dz
                copy = remote(
                    buf.at[k, source],
                    buf.at[k, source],
                    y_send.at[slot],
                    y_recv.at[slot],
                    chip_of(0, dy) * CORES + k,
                )
                copy.start()
                crossed.append((dz, dy, copy))
                pending.append(copy)

        def share(dz, dy):
            source = chip_of(nz - dz, ny - dy)
            slot = dy * nz + dz
            copy = remote(
                buf.at[k, source], buf.at[k, source], s_send.at[slot], s_recv.at[slot], sister
            )
            copy.start()
            shared.append(copy)
            pending.append(copy)

        cross(0)
        share(0, 0)
        for dz in range(1, nz):
            lines[dz - 1].wait_recv()
            cross(dz)
            share(dz, 0)
        for dz, dy, copy in crossed:
            copy.wait_recv()
            share(dz, dy)
        for copy in shared:
            copy.wait_recv()

    ld_k.wait()
    ld_v.wait()
    ld_q.wait()
    ld_coef.wait()
    kv_copies[0].wait_recv()
    kv_copies[1].wait_recv()
    kv_heads = kv_width // HD
    for g in range(kv_heads):
        vt[g] = jnp.transpose(vc[:, :, g * HD : (g + 1) * HD].reshape(CORES * here, HD))
    gather(coef, c_sems)
    for copy in q_second:
        copy.wait_recv()

    stat[...] = jnp.zeros_like(stat)
    seen = len_ref[...] - c * (CORES * here)
    stat_half = stat.shape[2] // 2

    def part_copies(jc, dk):
        order = lax.rem(c + 1 + jc, half_chips)
        owner = k * half_chips + order
        kt = lax.rem(k + dk, CORES)
        slot = jc * CORES + dk
        pairs = ((num.at[order, kt], rnum.at[c]), (stat.at[order, kt], rstat.at[c]))
        far = [
            remote(src, dst, a_send.at[i, slot], a_recv.at[i, c], owner * CORES + kt)
            for i, (src, dst) in enumerate(pairs)
        ]
        near = [
            pltpu.make_async_copy(src, dst, a_recv.at[i, c]) for i, (src, dst) in enumerate(pairs)
        ]
        return owner * CORES + kt != me, far, near

    def owner_step(jc, carry):
        order = lax.rem(c + 1 + jc, half_chips)

        def head_step(hh, carry):
            h = order * hpc + hh
            g = h // GROUP
            qh = q_all[:, :, :, pl.ds(pl.multiple_of(h * HD, 128), HD)].reshape(all_rows, HD)
            kh = kc[:, :, pl.ds(pl.multiple_of(g * HD, 128), HD)].reshape(CORES * here, HD)
            s = lax.dot_general(kh, qh, (((1,), (1,)), ((), ())), preferred_element_type=F32)
            place = lax.broadcasted_iota(jnp.int32, s.shape, 0)
            t = jnp.where(place < seen, s * SCALE2, NEG)
            m = jnp.maximum(jnp.max(t, axis=0, keepdims=True), FLOOR)
            p = jnp.exp2(t - m)
            total = jnp.sum(p, axis=0, keepdims=True)
            o = jnp.dot(vt[g], p.astype(BF16), preferred_element_type=F32).astype(BF16)
            at = pl.ds(pl.multiple_of(hh * HD, HD), HD)
            for kt in range(CORES):
                lanes = slice(kt * half_rows, (kt + 1) * half_rows)
                num[order, kt, at, :] = o[:, lanes]
                stat[order, kt, pl.ds(hh, 1), :] = m[:, lanes]
                stat[order, kt, pl.ds(stat_half + hh, 1), :] = total[:, lanes]
            return carry

        lax.fori_loop(0, hpc, head_step, 0)
        for dk in range(CORES):
            is_far, far, near = part_copies(jc, dk)

            @pl.when(is_far)
            def _():
                for copy in far:
                    copy.start()

            @pl.when(jnp.logical_not(is_far))
            def _():
                for copy in near:
                    copy.start()

        return carry

    lax.fori_loop(0, half_chips, owner_step, 0)

    ld_nv.wait()
    ld_fs.wait()
    ld_ow.wait()
    kv_copies[2].wait_recv()
    for copy in fresh_copies:
        copy.wait_recv()
    for i in range(chips):
        pltpu.make_async_copy(rnum.at[i], rnum.at[i], a_recv.at[0, i]).wait()
        pltpu.make_async_copy(rstat.at[i], rstat.at[i], a_recv.at[1, i]).wait()

    fresh_t = jnp.transpose(fsr[...].reshape(half_rows, HD))
    value_t = jnp.transpose(nvr[...].astype(F32).reshape(half_rows, HD))
    for hh in range(hpc):
        fresh = fresh_t[hh : hh + 1, :]
        peak = fresh
        for i in range(chips):
            peak = jnp.maximum(peak, rstat[i, hh : hh + 1, :])
        w = jnp.exp2(fresh - peak)
        den = w
        top = w * value_t
        for i in range(chips):
            w = jnp.exp2(rstat[i, hh : hh + 1, :] - peak)
            den = den + w * rstat[i, stat_half + hh : stat_half + hh + 1, :]
            top = top + w * rnum[i, hh * HD : (hh + 1) * HD, :].astype(F32)
        att[:, hh * HD : (hh + 1) * HD] = jnp.transpose(top / den).astype(BF16)

    tile = 512

    def project(i, carry):
        cols = pl.ds(pl.multiple_of(i * tile, 128), tile)
        weight = ow[:, :, cols].reshape(hpc * HD, tile)
        part = jnp.dot(att[...], weight, preferred_element_type=F32).astype(BF16)
        ost[:, :, cols] = part.reshape(chips, rows, tile)
        return carry

    lax.fori_loop(0, model // tile, project, 0)

    def send_home(src, dst, send, recv):
        copies = []
        for j in range(1, chips):
            target = lax.rem(c + j, chips)
            copy = remote(src.at[target], dst.at[c], send.at[j], recv.at[j], target * CORES + k)
            copy.start()
            copies.append(copy)
            pending.append(copy)
        total = src[c].astype(F32)
        for j in range(1, chips):
            copies[j - 1].wait_recv()
            total = total + dst[lax.rem(c + chips - j, chips)].astype(F32)
        return total

    after = (res_ref[...].astype(F32) + send_home(ost, r2, b_send, b_recv)).astype(BF16)
    aft[...] = after
    middle = after.astype(F32)
    inv = lax.rsqrt(jnp.mean(middle * middle, axis=-1, keepdims=True) + 1e-06)
    xn[k, c] = (middle * inv * gain_ref[...].astype(F32)).astype(BF16)
    gather(xn, x_sems)

    for copy in ld_w:
        copy.wait()
    ff = wg.shape[2]
    ftile = 256
    lane = lax.broadcasted_iota(jnp.int32, (all_rows, 128), 1)
    experts = wg.shape[0]
    for e in range(experts):

        def enter(i, carry):
            cols = pl.ds(pl.multiple_of(i * ftile, 128), ftile)
            x = xn[...].reshape(all_rows, model)
            gate = jnp.dot(x, wg[e, :, cols], preferred_element_type=F32)
            up = jnp.dot(x, wu[e, :, cols], preferred_element_type=F32)
            hid[:, cols] = (gate / (1.0 + jnp.exp(-gate)) * up).astype(BF16)
            return carry

        lax.fori_loop(0, ff // ftile, enter, 0)
        table = coef[...].reshape(all_rows, 128)
        share = jnp.sum(jnp.where(lane == me * experts + e, table, 0.0), axis=1, keepdims=True)

        def leave(i, carry):
            cols = pl.ds(pl.multiple_of(i * tile, 128), tile)
            made = jnp.dot(hid[...], wd[e, :, cols], preferred_element_type=F32)
            made = share * made.astype(BF16).astype(F32)
            if e == 0:
                acc[:, cols] = made
            else:
                acc[:, cols] += made
            return carry

        lax.fori_loop(0, model // tile, leave, 0)

    own_part = pl.ds(pl.multiple_of(k * half_rows, 128), half_rows)
    other_part = pl.ds(pl.multiple_of((1 - k) * half_rows, 128), half_rows)
    es[...] = acc[other_part, :].astype(BF16)
    swap = remote(es, er, e_sems.at[0], e_sems.at[1], sister)
    swap.start()
    pending.append(swap)
    swap.wait_recv()
    ost3[...] = (acc[own_part, :] + er[...].astype(F32)).astype(BF16).reshape(chips, rows, model)
    mixed = send_home(ost3, r3, d_send, d_recv)
    out_ref[...] = (aft[...].astype(F32) + mixed).astype(BF16)

    for copy in pending:
        copy.wait_send()

    def drain(jc, carry):
        for dk in range(CORES):
            is_far, far, near = part_copies(jc, dk)

            @pl.when(is_far)
            def _():
                for copy in far:
                    copy.wait_send()

        return carry

    lax.fori_loop(0, half_chips, drain, 0)


def on_device(
    ny,
    queries,
    new_key,
    new_value,
    key_cache,
    value_cache,
    cache_len,
    out_weight,
    residual,
    norm_gain,
    expert_ids,
    route_weight,
    w_gate,
    w_up,
    w_down,
):
    n = lax.axis_size("ctx")
    chips = n // CORES
    nz = chips // ny
    hpc = HEADS // chips
    rows = queries.shape[0]
    model = residual.shape[1]
    here = key_cache.shape[0]
    ff = w_gate.shape[2]
    all_rows, half_rows = n * rows, chips * rows
    width = queries.shape[1] // CORES
    kv_width = key_cache.shape[1] // CORES
    fresh = (
        jnp.einsum(
            "rgqd,rgd->rgq",
            queries.reshape(rows, KVH, GROUP, HD),
            new_key.reshape(rows, KVH, HD),
            preferred_element_type=F32,
        )
        * SCALE2
    )
    fresh = jnp.transpose(fresh.reshape(rows, chips, hpc), (1, 0, 2))
    fresh = jnp.pad(fresh, ((0, 0), (0, 0), (0, HD - hpc)))
    lane = jnp.arange(128, dtype=jnp.int32)
    coef = jnp.sum(
        jnp.where(expert_ids[:, :, None] == lane, route_weight[:, :, None], 0.0), axis=1
    )
    lens = jnp.transpose(cache_len.reshape(chips, CORES, rows), (1, 0, 2)).reshape(1, all_rows)
    stat_rows = max(8, 2 * hpc)
    any_space = pl.BlockSpec(memory_space=pl.ANY)
    vmem = pl.BlockSpec(memory_space=pltpu.VMEM)
    dma = lambda *dims: pltpu.SemaphoreType.DMA(dims)
    gather_sems = [dma(nz), dma(nz), dma(ny * nz), dma(ny * nz), dma(ny * nz), dma(ny * nz)]
    return pl.pallas_call(
        functools.partial(layer_kernel, n, ny),
        out_shape=jax.ShapeDtypeStruct((rows, model), BF16),
        in_specs=[any_space] * 6 + [vmem, any_space, vmem, vmem] + [any_space] * 3,
        out_specs=vmem,
        scratch_shapes=[
            pltpu.VMEM((CORES, chips, rows, width), BF16),
            pltpu.VMEM((CORES, here, kv_width), BF16),
            pltpu.VMEM((CORES, here, kv_width), BF16),
            pltpu.VMEM((kv_width // HD, HD, CORES * here), BF16),
            pltpu.VMEM((CORES, chips, rows, 128), F32),
            pltpu.VMEM((chips, rows, HD), BF16),
            pltpu.VMEM((chips, rows, HD), F32),
            pltpu.VMEM((chips // CORES, CORES, hpc * HD, half_rows), BF16),
            pltpu.VMEM((chips // CORES, CORES, stat_rows, half_rows), F32),
            pltpu.VMEM((chips, hpc * HD, half_rows), BF16),
            pltpu.VMEM((chips, stat_rows, half_rows), F32),
            pltpu.VMEM((CORES,) + out_weight.shape, BF16),
            pltpu.VMEM((half_rows, hpc * HD), BF16),
            pltpu.VMEM((chips, rows, model), BF16),
            pltpu.VMEM((chips, rows, model), BF16),
            pltpu.VMEM((CORES, chips, rows, model), BF16),
            pltpu.VMEM(w_gate.shape, BF16),
            pltpu.VMEM(w_up.shape, BF16),
            pltpu.VMEM(w_down.shape, BF16),
            pltpu.VMEM((all_rows, ff), BF16),
            pltpu.VMEM((all_rows, model), F32),
            pltpu.VMEM((half_rows, model), BF16),
            pltpu.VMEM((half_rows, model), BF16),
            pltpu.VMEM((chips, rows, model), BF16),
            pltpu.VMEM((chips, rows, model), BF16),
            pltpu.VMEM((rows, model), BF16),
            dma(10),
            dma(3),
            dma(3),
            dma(nz * CORES),
            dma(nz * CORES),
            dma(ny * nz * CORES),
            dma(ny * nz * CORES),
            gather_sems,
            dma(2, chips),
            dma(2, chips),
            dma(2, chips),
            dma(2, chips),
            dma(chips),
            dma(chips),
            gather_sems,
            dma(2),
            dma(chips),
            dma(chips),
        ],
        compiler_params=pltpu.CompilerParams(
            collective_id=0, has_side_effects=True, vmem_limit_bytes=60 * 1024 * 1024
        ),
    )(
        queries,
        new_value,
        fresh,
        coef,
        key_cache,
        value_cache,
        lens,
        out_weight,
        residual,
        norm_gain.reshape(1, model),
        w_gate,
        w_up,
        w_down,
    )


def solution(mesh):
    rowed = P(("groups", "ctx"), None)
    placed = (
        rowed,
        rowed,
        rowed,
        rowed,
        rowed,
        P("groups"),
        P("ctx", None),
        rowed,
        P(),
        rowed,
        rowed,
        P("ctx", None, None),
        P("ctx", None, None),
        P("ctx", None, None),
    )
    ny = max(1, 4 // mesh.shape["groups"])
    return jax.shard_map(
        functools.partial(on_device, ny),
        mesh=mesh,
        in_specs=placed,
        out_specs=rowed,
        check_vma=False,
    )
```

```python
import functools
import math

import jax
import jax.numpy as jnp
from jax import lax
from jax.experimental import pallas as pl
from jax.experimental.pallas import tpu as pltpu
from jax.sharding import PartitionSpec as P

HEADS = 32
KVH = 4
HD = 128
GROUP = HEADS // KVH
CORES = 2
NEG = -1e30
FLOOR = -1e29
MESH = pl.DeviceIdType.MESH
F32 = jnp.float32
BF16 = jnp.bfloat16
SCALE2 = math.log2(math.e) / math.sqrt(HD)


def remote(src, dst, send, recv, target):
    return pltpu.make_async_remote_copy(
        src_ref=src,
        dst_ref=dst,
        send_sem=send,
        recv_sem=recv,
        device_id={"ctx": target},
        device_id_type=MESH,
    )


def layer_kernel(
    n,
    ny,
    q_in,
    nk_ref,
    nv_in,
    ids_ref,
    share_ref,
    kc_in,
    vc_in,
    len_ref,
    ow_in,
    res_ref,
    gain_ref,
    wg_in,
    wu_in,
    wd_in,
    out_ref,
    q_all,
    kc,
    vc,
    vt,
    coef,
    nvr,
    fs,
    fsr,
    bias,
    num,
    stat,
    rnum,
    rstat,
    ow,
    att,
    ost,
    r2,
    xn,
    wg,
    wu,
    wd,
    hid,
    acc,
    es,
    er,
    ost3,
    r3,
    aft,
    load_sem,
    kv_send,
    kv_recv,
    q_send,
    q_recv,
    q_relay_send,
    q_relay_recv,
    c_sems,
    f_send,
    f_recv,
    a_send,
    a_recv,
    b_send,
    b_recv,
    x_sems,
    e_sems,
    d_send,
    d_recv,
):
    chips = n // CORES
    nz = chips // ny
    half_chips = chips // CORES
    hpc = HEADS // chips
    rows = q_in.shape[0]
    all_rows = n * rows
    half_rows = chips * rows
    width = q_in.shape[1] // CORES
    kv_width = kc_in.shape[1] // CORES
    here = kc_in.shape[0]
    model = res_ref.shape[1]
    me = lax.axis_index("ctx")
    k = lax.rem(me, CORES)
    c = me // CORES
    z = c // ny
    y = lax.rem(c, ny)
    sister = c * CORES + 1 - k

    def chip_of(dz, dy):
        return lax.rem(z + dz, nz) * ny + lax.rem(y + dy, ny)

    loads = []

    def load(src, dst):
        copy = pltpu.make_async_copy(src, dst, load_sem.at[len(loads)])
        copy.start()
        loads.append(copy)
        return copy

    own_cols = pl.ds(pl.multiple_of(k * kv_width, 128), kv_width)
    other_cols = pl.ds(pl.multiple_of((1 - k) * kv_width, 128), kv_width)
    ld_k = load(kc_in.at[:, own_cols], kc.at[k])
    ld_v = load(vc_in.at[:, own_cols], vc.at[k])
    chunk = hpc * HD

    def order_at(line, jc):
        return lax.rem(line + 1 + jc, half_chips)

    def q_cols(core, order):
        return pl.ds(pl.multiple_of(core * width + order * chunk, 128), chunk)

    ld_q = [
        load(q_in.at[:, q_cols(k, order)], q_all.at[order, k, c]) for order in range(half_chips)
    ]
    kv_head = (c * hpc) // GROUP
    ld_nv = load(
        nv_in.at[:, pl.ds(pl.multiple_of(kv_head * HD, 128), HD)], nvr.at[c]
    )
    ld_ow = load(ow_in, ow.at[k])

    barrier = pltpu.get_barrier_semaphore()
    for i in range(1, n):
        pl.semaphore_signal(
            barrier, inc=1, device_id={"ctx": lax.rem(me + i, n)}, device_id_type=MESH
        )
    pl.semaphore_wait(barrier, n - 1)

    pending = []

    kv_copies = []
    for i, (src, dst) in enumerate(
        ((kc_in.at[:, other_cols], kc.at[k]), (vc_in.at[:, other_cols], vc.at[k]), (ow_in, ow.at[k]))
    ):
        copy = remote(src, dst, kv_send.at[i], kv_recv.at[i], sister)
        copy.start()
        kv_copies.append(copy)
        pending.append(copy)

    lines = [(dz, dk) for dz in range(nz) for dk in range(CORES) if (dz, dk) != (0, 0)]

    def q_line(jc, dz, dk):
        kt = lax.rem(k + dk, CORES)
        order = order_at(lax.rem(z + dz, nz), jc)
        slot = dz * CORES + dk
        return remote(
            q_in.at[:, q_cols(kt, order)],
            q_all.at[order, k, c],
            q_send.at[jc, slot],
            q_recv.at[jc, slot],
            chip_of(dz, 0) * CORES + kt,
        )

    def q_cross(jc, dz, dk, dy):
        order = order_at(z, jc)
        core, chip = lax.rem(k + dk, CORES), chip_of(nz - dz, 0)
        held = q_all.at[order, core, chip]
        src = q_in.at[:, q_cols(k, order)] if (dz, dk) == (0, 0) else held
        slot = ((dy - 1) * nz + dz) * CORES + dk
        return remote(
            src,
            held,
            q_relay_send.at[jc, slot],
            q_relay_recv.at[jc, slot],
            chip_of(0, dy) * CORES + k,
        )

    def q_send_all(jc):
        for dy in range(1, ny):
            q_cross(jc, 0, 0, dy).start()
        for dz, dk in lines:
            q_line(jc, dz, dk).start()

    def q_relay(jc):
        for dz, dk in lines:
            q_line(jc, dz, dk).wait_recv()
            for dy in range(1, ny):
                q_cross(jc, dz, dk, dy).start()

    def q_arrive(jc):
        for dy in range(1, ny):
            for dz, dk in [(0, 0)] + lines:
                q_cross(jc, dz, dk, dy).wait_recv()

    for jc in range(half_chips):
        q_send_all(jc)

    lane = lax.broadcasted_iota(jnp.int32, (rows, 128), 1)
    for chip in range(chips):
        tile = jnp.zeros((rows, 128), F32)
        for hh in range(hpc):
            h = chip * hpc + hh
            g = h // GROUP
            qv = q_in[:, h * HD : (h + 1) * HD].astype(F32)
            kv = nk_ref[:, g * HD : (g + 1) * HD].astype(F32)
            score = jnp.sum(qv * kv, axis=1, keepdims=True) * SCALE2
            tile = jnp.where(lane == hh, score, tile)
        fs[chip] = tile
    table = jnp.zeros((rows, 128), F32)
    for t in range(ids_ref.shape[1]):
        table = table + jnp.where(lane == ids_ref[:, t : t + 1], share_ref[:, t : t + 1], 0.0)
    coef[k, c] = table
    fsr[c] = fs[c]

    fresh_copies = []
    for j in range(1, chips):
        target = lax.rem(c + j, chips)
        cols = pl.ds(pl.multiple_of(((target * hpc) // GROUP) * HD, 128), HD)
        for i, (src, dst) in enumerate(((nv_in.at[:, cols], nvr.at[c]), (fs.at[target], fsr.at[c]))):
            copy = remote(src, dst, f_send.at[i, j], f_recv.at[i, j], target * CORES + k)
            copy.start()
            fresh_copies.append(copy)
            pending.append(copy)

    for src, dst in ((wg_in, wg), (wu_in, wu), (wd_in, wd)):
        load(src, dst)
    ld_w = loads[-3:]

    def gather(buf, sems):
        z_send, z_recv, y_send, y_recv, s_send, s_recv = sems
        along = []
        for dz in range(1, nz):
            copy = remote(
                buf.at[k, c], buf.at[k, c], z_send.at[dz], z_recv.at[dz], chip_of(dz, 0) * CORES + k
            )
            copy.start()
            along.append(copy)
            pending.append(copy)
        crossed, shared = [], []

        def cross(dz):
            source = chip_of(nz - dz, 0)
            for dy in range(1, ny):
                slot = dy * nz + dz
                copy = remote(
                    buf.at[k, source],
                    buf.at[k, source],
                    y_send.at[slot],
                    y_recv.at[slot],
                    chip_of(0, dy) * CORES + k,
                )
                copy.start()
                crossed.append((dz, dy, copy))
                pending.append(copy)

        def share(dz, dy):
            source = chip_of(nz - dz, ny - dy)
            slot = dy * nz + dz
            copy = remote(
                buf.at[k, source], buf.at[k, source], s_send.at[slot], s_recv.at[slot], sister
            )
            copy.start()
            shared.append(copy)
            pending.append(copy)

        cross(0)
        share(0, 0)
        for dz in range(1, nz):
            along[dz - 1].wait_recv()
            cross(dz)
            share(dz, 0)
        for dz, dy, copy in crossed:
            copy.wait_recv()
            share(dz, dy)
        for copy in shared:
            copy.wait_recv()

    ld_k.wait()
    ld_v.wait()
    for copy in ld_q:
        copy.wait()
    kv_copies[0].wait_recv()
    kv_copies[1].wait_recv()
    kv_heads = kv_width // HD
    for g in range(kv_heads):
        vt[g, :HD] = jnp.transpose(vc[:, :, g * HD : (g + 1) * HD].reshape(CORES * here, HD))
        vt[g, HD:] = jnp.ones((vt.shape[1] - HD, CORES * here), BF16)

    stat[...] = jnp.zeros_like(stat)
    seen = len_ref[...] - c * (CORES * here)
    place = lax.broadcasted_iota(jnp.int32, bias.shape, 0)
    bias[...] = jnp.where(place < seen, 0.0, NEG)
    q_relay(0)
    stat_half = stat.shape[2] // 2

    def part_copies(jc, dk):
        order = order_at(z, jc)
        owner = k * half_chips + order
        kt = lax.rem(k + dk, CORES)
        slot = jc * CORES + dk
        pairs = ((num.at[order, kt], rnum.at[c]), (stat.at[order, kt], rstat.at[c]))
        far = [
            remote(src, dst, a_send.at[i, slot], a_recv.at[i, c], owner * CORES + kt)
            for i, (src, dst) in enumerate(pairs)
        ]
        near = [
            pltpu.make_async_copy(src, dst, a_recv.at[i, c]) for i, (src, dst) in enumerate(pairs)
        ]
        return owner * CORES + kt != me, far, near

    def owner_step(jc, carry):
        order = order_at(z, jc)

        q_arrive(jc)

        def scores(hh):
            g = (order * hpc + hh) // GROUP
            at = pl.ds(pl.multiple_of(hh * HD, HD), HD)
            qh = q_all[order, :, :, :, at].reshape(all_rows, HD)
            kh = kc[:, :, pl.ds(pl.multiple_of(g * HD, 128), HD)].reshape(CORES * here, HD)
            s = lax.dot_general(kh, qh, (((1,), (1,)), ((), ())), preferred_element_type=F32)
            return g, s * SCALE2 + bias[...]

        def finish(hh, g, t):
            m = jnp.maximum(jnp.max(t, axis=0, keepdims=True), FLOOR)
            p = jnp.exp2(t - m).astype(BF16)
            o = jnp.dot(vt[g], p, preferred_element_type=F32)
            total = o[HD : HD + 1, :]
            o = o[:HD, :].astype(BF16)
            at = pl.ds(pl.multiple_of(hh * HD, HD), HD)
            for kt in range(CORES):
                cut = slice(kt * half_rows, (kt + 1) * half_rows)
                num[order, kt, at, :] = o[:, cut]
                stat[order, kt, pl.ds(hh, 1), :] = m[:, cut]
                stat[order, kt, pl.ds(stat_half + hh, 1), :] = total[:, cut]

        pairs = hpc // 2

        def head_step(i, carry):
            @pl.when(jnp.logical_and(i == pairs // 2, jc + 1 < half_chips))
            def _():
                q_relay(jc + 1)

            both = [(2 * i + u, *scores(2 * i + u)) for u in range(2)]
            for hh, g, t in both:
                finish(hh, g, t)
            return carry

        lax.fori_loop(0, pairs, head_step, 0)
        for dk in range(CORES):
            is_far, far, near = part_copies(jc, dk)

            @pl.when(is_far)
            def _():
                for copy in far:
                    copy.start()

            @pl.when(jnp.logical_not(is_far))
            def _():
                for copy in near:
                    copy.start()

        return carry

    lax.fori_loop(0, half_chips, owner_step, 0)

    gather(coef, c_sems)
    ld_nv.wait()
    ld_ow.wait()
    kv_copies[2].wait_recv()
    for copy in fresh_copies:
        copy.wait_recv()
    for i in range(chips):
        pltpu.make_async_copy(rnum.at[i], rnum.at[i], a_recv.at[0, i]).wait()
        pltpu.make_async_copy(rstat.at[i], rstat.at[i], a_recv.at[1, i]).wait()

    fresh_t = jnp.transpose(fsr[...].reshape(half_rows, HD))
    value_t = jnp.transpose(nvr[...].astype(F32).reshape(half_rows, HD))
    for hh in range(hpc):
        fresh = fresh_t[hh : hh + 1, :]
        peak = fresh
        for i in range(chips):
            peak = jnp.maximum(peak, rstat[i, hh : hh + 1, :])
        w = jnp.exp2(fresh - peak)
        den = w
        top = w * value_t
        for i in range(chips):
            w = jnp.exp2(rstat[i, hh : hh + 1, :] - peak)
            den = den + w * rstat[i, stat_half + hh : stat_half + hh + 1, :]
            top = top + w * rnum[i, hh * HD : (hh + 1) * HD, :].astype(F32)
        att[:, hh * HD : (hh + 1) * HD] = jnp.transpose(top / den).astype(BF16)

    tile = 512

    def project(i, carry):
        cols = pl.ds(pl.multiple_of(i * tile, 128), tile)
        weight = ow[:, :, cols].reshape(hpc * HD, tile)
        part = jnp.dot(att[...], weight, preferred_element_type=F32).astype(BF16)
        ost[:, :, cols] = part.reshape(chips, rows, tile)
        return carry

    lax.fori_loop(0, model // tile, project, 0)

    def send_home(src, dst, send, recv):
        copies = []
        for j in range(1, chips):
            target = lax.rem(c + j, chips)
            copy = remote(src.at[target], dst.at[c], send.at[j], recv.at[j], target * CORES + k)
            copy.start()
            copies.append(copy)
            pending.append(copy)
        total = src[c].astype(F32)
        for j in range(1, chips):
            copies[j - 1].wait_recv()
            total = total + dst[lax.rem(c + chips - j, chips)].astype(F32)
        return total

    after = (res_ref[...].astype(F32) + send_home(ost, r2, b_send, b_recv)).astype(BF16)
    aft[...] = after
    middle = after.astype(F32)
    inv = lax.rsqrt(jnp.mean(middle * middle, axis=-1, keepdims=True) + 1e-06)
    xn[k, c] = (middle * inv * gain_ref[...].astype(F32).reshape(1, model)).astype(BF16)
    gather(xn, x_sems)

    for copy in ld_w:
        copy.wait()
    ff = wg.shape[2]
    ftile = 256
    lane = lax.broadcasted_iota(jnp.int32, (all_rows, 128), 1)
    experts = wg.shape[0]
    for e in range(experts):

        def enter(i, carry):
            cols = pl.ds(pl.multiple_of(i * ftile, 128), ftile)
            x = xn[...].reshape(all_rows, model)
            gate = jnp.dot(x, wg[e, :, cols], preferred_element_type=F32)
            up = jnp.dot(x, wu[e, :, cols], preferred_element_type=F32)
            hid[:, cols] = (gate / (1.0 + jnp.exp(-gate)) * up).astype(BF16)
            return carry

        lax.fori_loop(0, ff // ftile, enter, 0)
        table = coef[...].reshape(all_rows, 128)
        share = jnp.sum(jnp.where(lane == me * experts + e, table, 0.0), axis=1, keepdims=True)

        def leave(i, carry):
            cols = pl.ds(pl.multiple_of(i * tile, 128), tile)
            made = jnp.dot(hid[...], wd[e, :, cols], preferred_element_type=F32)
            made = share * made.astype(BF16).astype(F32)
            if e == 0:
                acc[:, cols] = made
            else:
                acc[:, cols] += made
            return carry

        lax.fori_loop(0, model // tile, leave, 0)

    own_part = pl.ds(pl.multiple_of(k * half_rows, 128), half_rows)
    other_part = pl.ds(pl.multiple_of((1 - k) * half_rows, 128), half_rows)
    es[...] = acc[other_part, :].astype(BF16)
    swap = remote(es, er, e_sems.at[0], e_sems.at[1], sister)
    swap.start()
    pending.append(swap)
    swap.wait_recv()
    ost3[...] = (acc[own_part, :] + er[...].astype(F32)).astype(BF16).reshape(chips, rows, model)
    mixed = send_home(ost3, r3, d_send, d_recv)
    out_ref[...] = (aft[...].astype(F32) + mixed).astype(BF16)

    for copy in pending:
        copy.wait_send()

    def drain(jc, carry):
        for dz, dk in lines:
            q_line(jc, dz, dk).wait_send()
        for dy in range(1, ny):
            for dz, dk in [(0, 0)] + lines:
                q_cross(jc, dz, dk, dy).wait_send()
        for dk in range(CORES):
            is_far, far, near = part_copies(jc, dk)

            @pl.when(is_far)
            def _():
                for copy in far:
                    copy.wait_send()

        return carry

    lax.fori_loop(0, half_chips, drain, 0)


def on_device(
    ny,
    queries,
    new_key,
    new_value,
    key_cache,
    value_cache,
    cache_len,
    out_weight,
    residual,
    norm_gain,
    expert_ids,
    route_weight,
    w_gate,
    w_up,
    w_down,
):
    n = lax.axis_size("ctx")
    chips = n // CORES
    nz = chips // ny
    hpc = HEADS // chips
    rows = queries.shape[0]
    model = residual.shape[1]
    here = key_cache.shape[0]
    ff = w_gate.shape[2]
    all_rows, half_rows = n * rows, chips * rows
    half_chips = chips // CORES
    kv_width = key_cache.shape[1] // CORES
    lens = jnp.transpose(cache_len.reshape(chips, CORES, rows), (1, 0, 2)).reshape(1, all_rows)
    stat_rows = max(8, 2 * hpc)
    any_space = pl.BlockSpec(memory_space=pl.ANY)
    vmem = pl.BlockSpec(memory_space=pltpu.VMEM)
    dma = lambda *dims: pltpu.SemaphoreType.DMA(dims)
    gather_sems = [dma(nz), dma(nz), dma(ny * nz), dma(ny * nz), dma(ny * nz), dma(ny * nz)]
    return pl.pallas_call(
        functools.partial(layer_kernel, n, ny),
        out_shape=jax.ShapeDtypeStruct((rows, model), BF16),
        in_specs=[vmem] * 5 + [any_space] * 2 + [vmem, any_space, vmem, vmem] + [any_space] * 3,
        out_specs=vmem,
        scratch_shapes=[
            pltpu.VMEM((half_chips, CORES, chips, rows, hpc * HD), BF16),
            pltpu.VMEM((CORES, here, kv_width), BF16),
            pltpu.VMEM((CORES, here, kv_width), BF16),
            pltpu.VMEM((kv_width // HD, HD + 16, CORES * here), BF16),
            pltpu.VMEM((CORES, chips, rows, 128), F32),
            pltpu.VMEM((chips, rows, HD), BF16),
            pltpu.VMEM((chips, rows, HD), F32),
            pltpu.VMEM((chips, rows, HD), F32),
            pltpu.VMEM((CORES * here, all_rows), F32),
            pltpu.VMEM((chips // CORES, CORES, hpc * HD, half_rows), BF16),
            pltpu.VMEM((chips // CORES, CORES, stat_rows, half_rows), F32),
            pltpu.VMEM((chips, hpc * HD, half_rows), BF16),
            pltpu.VMEM((chips, stat_rows, half_rows), F32),
            pltpu.VMEM((CORES,) + out_weight.shape, BF16),
            pltpu.VMEM((half_rows, hpc * HD), BF16),
            pltpu.VMEM((chips, rows, model), BF16),
            pltpu.VMEM((chips, rows, model), BF16),
            pltpu.VMEM((CORES, chips, rows, model), BF16),
            pltpu.VMEM(w_gate.shape, BF16),
            pltpu.VMEM(w_up.shape, BF16),
            pltpu.VMEM(w_down.shape, BF16),
            pltpu.VMEM((all_rows, ff), BF16),
            pltpu.VMEM((all_rows, model), F32),
            pltpu.VMEM((half_rows, model), BF16),
            pltpu.VMEM((half_rows, model), BF16),
            pltpu.VMEM((chips, rows, model), BF16),
            pltpu.VMEM((chips, rows, model), BF16),
            pltpu.VMEM((rows, model), BF16),
            dma(half_chips + 8),
            dma(3),
            dma(3),
            dma(half_chips, nz * CORES),
            dma(half_chips, nz * CORES),
            dma(half_chips, ny * nz * CORES),
            dma(half_chips, ny * nz * CORES),
            gather_sems,
            dma(2, chips),
            dma(2, chips),
            dma(2, chips),
            dma(2, chips),
            dma(chips),
            dma(chips),
            gather_sems,
            dma(2),
            dma(chips),
            dma(chips),
        ],
        compiler_params=pltpu.CompilerParams(
            collective_id=0, has_side_effects=True, vmem_limit_bytes=60 * 1024 * 1024
        ),
    )(
        queries,
        new_key,
        new_value,
        expert_ids,
        route_weight,
        key_cache,
        value_cache,
        lens,
        out_weight,
        residual,
        norm_gain,
        w_gate,
        w_up,
        w_down,
    )


def solution(mesh):
    rowed = P(("groups", "ctx"), None)
    placed = (
        rowed,
        rowed,
        rowed,
        rowed,
        rowed,
        P("groups"),
        P("ctx", None),
        rowed,
        P(),
        rowed,
        rowed,
        P("ctx", None, None),
        P("ctx", None, None),
        P("ctx", None, None),
    )
    ny = max(1, 4 // mesh.shape["groups"])
    return jax.shard_map(
        functools.partial(on_device, ny),
        mesh=mesh,
        in_specs=placed,
        out_specs=rowed,
        check_vma=False,
    )
```

```python
import functools
import math

import jax
import jax.numpy as jnp
from jax import lax
from jax.experimental import pallas as pl
from jax.experimental.pallas import tpu as pltpu
from jax.sharding import PartitionSpec as P

HEADS = 32
KVH = 4
HD = 128
GROUP = HEADS // KVH
CORES = 2
NEG = -1e30
FLOOR = -1e29
MESH = pl.DeviceIdType.MESH
F32 = jnp.float32
BF16 = jnp.bfloat16
SCALE2 = math.log2(math.e) / math.sqrt(HD)


def remote(src, dst, send, recv, target):
    return pltpu.make_async_remote_copy(
        src_ref=src,
        dst_ref=dst,
        send_sem=send,
        recv_sem=recv,
        device_id={"ctx": target},
        device_id_type=MESH,
    )


def layer_kernel(
    n,
    ny,
    q_in,
    nk_ref,
    nv_in,
    ids_ref,
    share_ref,
    kc_in,
    vc_in,
    len_ref,
    ow_in,
    res_ref,
    gain_ref,
    wg_in,
    wu_in,
    wd_in,
    out_ref,
    q_all,
    kc,
    vc,
    vt,
    coef,
    nvr,
    fs,
    fsr,
    bias,
    num,
    stat,
    ynum,
    ystat,
    mnum,
    mstat,
    rnum,
    rstat,
    ow,
    att,
    ost,
    y2,
    mid2,
    r2,
    xn,
    wg,
    wu,
    wd,
    hid,
    acc,
    es,
    er,
    ost3,
    y3,
    mid3,
    r3,
    aft,
    load_sem,
    kv_send,
    kv_recv,
    q_send,
    q_recv,
    q_relay_send,
    q_relay_recv,
    c_sems,
    f_send,
    f_recv,
    ya_send,
    ya_recv,
    a_send,
    a_recv,
    yb_send,
    yb_recv,
    b_send,
    b_recv,
    x_sems,
    e_sems,
    yd_send,
    yd_recv,
    d_send,
    d_recv,
):
    chips = n // CORES
    nz = chips // ny
    half_chips = chips // CORES
    hpc = HEADS // chips
    rows = q_in.shape[0]
    all_rows = n * rows
    half_rows = chips * rows
    width = q_in.shape[1] // CORES
    kv_width = kc_in.shape[1] // CORES
    here = kc_in.shape[0]
    model = res_ref.shape[1]
    me = lax.axis_index("ctx")
    k = lax.rem(me, CORES)
    c = me // CORES
    z = c // ny
    y = lax.rem(c, ny)
    sister = c * CORES + 1 - k

    def chip_of(dz, dy):
        return lax.rem(z + dz, nz) * ny + lax.rem(y + dy, ny)

    loads = []

    def load(src, dst):
        copy = pltpu.make_async_copy(src, dst, load_sem.at[len(loads)])
        copy.start()
        loads.append(copy)
        return copy

    own_cols = pl.ds(pl.multiple_of(k * kv_width, 128), kv_width)
    other_cols = pl.ds(pl.multiple_of((1 - k) * kv_width, 128), kv_width)
    ld_k = load(kc_in.at[:, own_cols], kc.at[k])
    ld_v = load(vc_in.at[:, own_cols], vc.at[k])
    chunk = hpc * HD

    across = chip_of(0, 1) * CORES + k

    def order_at(line, jc):
        return lax.rem(line + 1 + jc // ny, half_chips // ny) * ny + lax.rem(jc, ny)

    def q_cols(core, order):
        return pl.ds(pl.multiple_of(core * width + order * chunk, 128), chunk)

    ld_q = [
        load(q_in.at[:, q_cols(k, order)], q_all.at[order, k, c]) for order in range(half_chips)
    ]
    kv_head = (c * hpc) // GROUP
    ld_nv = load(
        nv_in.at[:, pl.ds(pl.multiple_of(kv_head * HD, 128), HD)], nvr.at[c]
    )
    ld_ow = load(ow_in, ow.at[k])

    barrier = pltpu.get_barrier_semaphore()
    for i in range(1, n):
        pl.semaphore_signal(
            barrier, inc=1, device_id={"ctx": lax.rem(me + i, n)}, device_id_type=MESH
        )
    pl.semaphore_wait(barrier, n - 1)

    pending = []

    kv_copies = []
    for i, (src, dst) in enumerate(
        ((kc_in.at[:, other_cols], kc.at[k]), (vc_in.at[:, other_cols], vc.at[k]), (ow_in, ow.at[k]))
    ):
        copy = remote(src, dst, kv_send.at[i], kv_recv.at[i], sister)
        copy.start()
        kv_copies.append(copy)
        pending.append(copy)

    lines = [(dz, dk) for dz in range(nz) for dk in range(CORES) if (dz, dk) != (0, 0)]

    def q_line(jc, dz, dk):
        kt = lax.rem(k + dk, CORES)
        order = order_at(lax.rem(z + dz, nz), jc)
        slot = dz * CORES + dk
        return remote(
            q_in.at[:, q_cols(kt, order)],
            q_all.at[order, k, c],
            q_send.at[jc, slot],
            q_recv.at[jc, slot],
            chip_of(dz, 0) * CORES + kt,
        )

    def q_cross(jc, dz, dk, dy):
        order = order_at(z, jc)
        core, chip = lax.rem(k + dk, CORES), chip_of(nz - dz, 0)
        held = q_all.at[order, core, chip]
        src = q_in.at[:, q_cols(k, order)] if (dz, dk) == (0, 0) else held
        slot = ((dy - 1) * nz + dz) * CORES + dk
        return remote(
            src,
            held,
            q_relay_send.at[jc, slot],
            q_relay_recv.at[jc, slot],
            chip_of(0, dy) * CORES + k,
        )

    def q_send_all(jc):
        for dy in range(1, ny):
            q_cross(jc, 0, 0, dy).start()
        for dz, dk in lines:
            q_line(jc, dz, dk).start()

    def q_relay(jc):
        for dz, dk in lines:
            q_line(jc, dz, dk).wait_recv()
            for dy in range(1, ny):
                q_cross(jc, dz, dk, dy).start()

    def q_arrive(jc):
        for dy in range(1, ny):
            for dz, dk in [(0, 0)] + lines:
                q_cross(jc, dz, dk, dy).wait_recv()

    for jc in range(half_chips):
        q_send_all(jc)

    lane = lax.broadcasted_iota(jnp.int32, (rows, 128), 1)
    for chip in range(chips):
        tile = jnp.zeros((rows, 128), F32)
        for hh in range(hpc):
            h = chip * hpc + hh
            g = h // GROUP
            qv = q_in[:, h * HD : (h + 1) * HD].astype(F32)
            kv = nk_ref[:, g * HD : (g + 1) * HD].astype(F32)
            score = jnp.sum(qv * kv, axis=1, keepdims=True) * SCALE2
            tile = jnp.where(lane == hh, score, tile)
        fs[chip] = tile
    table = jnp.zeros((rows, 128), F32)
    for t in range(ids_ref.shape[1]):
        table = table + jnp.where(lane == ids_ref[:, t : t + 1], share_ref[:, t : t + 1], 0.0)
    coef[k, c] = table
    fsr[c] = fs[c]

    fresh_copies = []
    for j in range(1, chips):
        target = lax.rem(c + j, chips)
        cols = pl.ds(pl.multiple_of(((target * hpc) // GROUP) * HD, 128), HD)
        for i, (src, dst) in enumerate(((nv_in.at[:, cols], nvr.at[c]), (fs.at[target], fsr.at[c]))):
            copy = remote(src, dst, f_send.at[i, j], f_recv.at[i, j], target * CORES + k)
            copy.start()
            fresh_copies.append(copy)
            pending.append(copy)

    for src, dst in ((wg_in, wg), (wu_in, wu), (wd_in, wd)):
        load(src, dst)
    ld_w = loads[-3:]

    def gather(buf, sems):
        z_send, z_recv, y_send, y_recv, s_send, s_recv = sems
        along = []
        for dz in range(1, nz):
            copy = remote(
                buf.at[k, c], buf.at[k, c], z_send.at[dz], z_recv.at[dz], chip_of(dz, 0) * CORES + k
            )
            copy.start()
            along.append(copy)
            pending.append(copy)
        crossed, shared = [], []

        def cross(dz):
            source = chip_of(nz - dz, 0)
            for dy in range(1, ny):
                slot = dy * nz + dz
                copy = remote(
                    buf.at[k, source],
                    buf.at[k, source],
                    y_send.at[slot],
                    y_recv.at[slot],
                    chip_of(0, dy) * CORES + k,
                )
                copy.start()
                crossed.append((dz, dy, copy))
                pending.append(copy)

        def share(dz, dy):
            source = chip_of(nz - dz, ny - dy)
            slot = dy * nz + dz
            copy = remote(
                buf.at[k, source], buf.at[k, source], s_send.at[slot], s_recv.at[slot], sister
            )
            copy.start()
            shared.append(copy)
            pending.append(copy)

        cross(0)
        share(0, 0)
        for dz in range(1, nz):
            along[dz - 1].wait_recv()
            cross(dz)
            share(dz, 0)
        for dz, dy, copy in crossed:
            copy.wait_recv()
            share(dz, dy)
        for copy in shared:
            copy.wait_recv()

    ld_k.wait()
    ld_v.wait()
    for copy in ld_q:
        copy.wait()
    kv_copies[0].wait_recv()
    kv_copies[1].wait_recv()
    kv_heads = kv_width // HD
    for g in range(kv_heads):
        vt[g, :HD] = jnp.transpose(vc[:, :, g * HD : (g + 1) * HD].reshape(CORES * here, HD))
        vt[g, HD:] = jnp.ones((vt.shape[1] - HD, CORES * here), BF16)

    stat[...] = jnp.zeros_like(stat)
    seen = len_ref[...] - c * (CORES * here)
    place = lax.broadcasted_iota(jnp.int32, bias.shape, 0)
    bias[...] = jnp.where(place < seen, 0.0, NEG)
    q_relay(0)
    stat_half = stat.shape[2] // 2

    def part_copies(jc, dk):
        order = order_at(z, jc)
        owner = k * half_chips + order
        kt = lax.rem(k + dk, CORES)
        slot = jc * CORES + dk
        if ny > 1:
            held = (mnum.at[order // ny, kt], mstat.at[order // ny, kt])
        else:
            held = (num.at[order, kt], stat.at[order, kt])
        pairs = tuple(zip(held, (rnum.at[z], rstat.at[z])))
        far = [
            remote(src, dst, a_send.at[i, slot], a_recv.at[i, z], owner * CORES + kt)
            for i, (src, dst) in enumerate(pairs)
        ]
        near = [
            pltpu.make_async_copy(src, dst, a_recv.at[i, z]) for i, (src, dst) in enumerate(pairs)
        ]
        return owner * CORES + kt != me, far, near

    def part_start(jc):
        for dk in range(CORES):
            is_far, far, near = part_copies(jc, dk)

            @pl.when(is_far)
            def _():
                for copy in far:
                    copy.start()

            @pl.when(jnp.logical_not(is_far))
            def _():
                for copy in near:
                    copy.start()

    def part_cross(jc):
        order = order_at(z, jc)
        pair = order // ny
        return [
            remote(src.at[order], dst.at[pair], ya_send.at[i, pair], ya_recv.at[i, pair], across)
            for i, (src, dst) in enumerate(((num, ynum), (stat, ystat)))
        ]

    def is_mine(jc):
        return lax.rem(order_at(z, jc), ny) == y

    def part_merge(jc):
        order = order_at(z, jc)
        pair = order // ny
        for copy in part_cross(jc):
            copy.wait_recv()
        for kt in range(CORES):
            for hh in range(hpc):
                cut = slice(hh * HD, (hh + 1) * HD)
                m1, l1 = (stat[order, kt, r : r + 1, :] for r in (hh, stat_half + hh))
                m2, l2 = (ystat[pair, kt, r : r + 1, :] for r in (hh, stat_half + hh))
                m = jnp.maximum(m1, m2)
                w1, w2 = jnp.exp2(m1 - m), jnp.exp2(m2 - m)
                mnum[pair, kt, cut, :] = (
                    w1 * num[order, kt, cut, :].astype(F32)
                    + w2 * ynum[pair, kt, cut, :].astype(F32)
                ).astype(BF16)
                mstat[pair, kt, hh : hh + 1, :] = m
                mstat[pair, kt, stat_half + hh : stat_half + hh + 1, :] = w1 * l1 + w2 * l2
        part_start(jc)

    def owner_step(jc, carry):
        order = order_at(z, jc)

        q_arrive(jc)

        def scores(hh):
            g = (order * hpc + hh) // GROUP
            at = pl.ds(pl.multiple_of(hh * HD, HD), HD)
            qh = q_all[order, :, :, :, at].reshape(all_rows, HD)
            kh = kc[:, :, pl.ds(pl.multiple_of(g * HD, 128), HD)].reshape(CORES * here, HD)
            s = lax.dot_general(kh, qh, (((1,), (1,)), ((), ())), preferred_element_type=F32)
            return g, s * SCALE2 + bias[...]

        def finish(hh, g, t):
            m = jnp.maximum(jnp.max(t, axis=0, keepdims=True), FLOOR)
            p = jnp.exp2(t - m).astype(BF16)
            o = jnp.dot(vt[g], p, preferred_element_type=F32)
            total = o[HD : HD + 1, :]
            o = o[:HD, :].astype(BF16)
            at = pl.ds(pl.multiple_of(hh * HD, HD), HD)
            for kt in range(CORES):
                cut = slice(kt * half_rows, (kt + 1) * half_rows)
                num[order, kt, at, :] = o[:, cut]
                stat[order, kt, pl.ds(hh, 1), :] = m[:, cut]
                stat[order, kt, pl.ds(stat_half + hh, 1), :] = total[:, cut]

        pairs = hpc // 2

        def head_step(i, carry):
            @pl.when(jnp.logical_and(i == pairs // 2, jc + 1 < half_chips))
            def _():
                q_relay(jc + 1)

            both = [(2 * i + u, *scores(2 * i + u)) for u in range(2)]
            for hh, g, t in both:
                finish(hh, g, t)
            return carry

        lax.fori_loop(0, pairs, head_step, 0)
        if ny == 1:
            part_start(jc)
            return carry

        @pl.when(jnp.logical_not(is_mine(jc)))
        def _():
            for copy in part_cross(jc):
                copy.start()

        before = jnp.maximum(jc - 1, 0)

        @pl.when(jnp.logical_and(jc > 0, is_mine(before)))
        def _():
            part_merge(before)

        return carry

    lax.fori_loop(0, half_chips, owner_step, 0)
    if ny > 1:

        @pl.when(is_mine(half_chips - 1))
        def _():
            part_merge(half_chips - 1)

    gather(coef, c_sems)
    ld_nv.wait()
    ld_ow.wait()
    kv_copies[2].wait_recv()
    for copy in fresh_copies:
        copy.wait_recv()
    for i in range(nz):
        pltpu.make_async_copy(rnum.at[i], rnum.at[i], a_recv.at[0, i]).wait()
        pltpu.make_async_copy(rstat.at[i], rstat.at[i], a_recv.at[1, i]).wait()

    fresh_t = jnp.transpose(fsr[...].reshape(half_rows, HD))
    value_t = jnp.transpose(nvr[...].astype(F32).reshape(half_rows, HD))
    for hh in range(hpc):
        fresh = fresh_t[hh : hh + 1, :]
        peak = fresh
        for i in range(nz):
            peak = jnp.maximum(peak, rstat[i, hh : hh + 1, :])
        w = jnp.exp2(fresh - peak)
        den = w
        top = w * value_t
        for i in range(nz):
            w = jnp.exp2(rstat[i, hh : hh + 1, :] - peak)
            den = den + w * rstat[i, stat_half + hh : stat_half + hh + 1, :]
            top = top + w * rnum[i, hh * HD : (hh + 1) * HD, :].astype(F32)
        att[:, hh * HD : (hh + 1) * HD] = jnp.transpose(top / den).astype(BF16)

    tile = 512

    def project(i, carry):
        cols = pl.ds(pl.multiple_of(i * tile, 128), tile)
        weight = ow[:, :, cols].reshape(hpc * HD, tile)
        part = jnp.dot(att[...], weight, preferred_element_type=F32).astype(BF16)
        ost[:, :, cols] = part.reshape(chips, rows, tile)
        return carry

    lax.fori_loop(0, model // tile, project, 0)

    def send_home(src, over, mid, dst, over_send, over_recv, send, recv):
        crossing = {}
        if ny > 1:
            for dz in [*range(1, nz), 0]:
                copy = remote(
                    src.at[chip_of(dz, 1)], over.at[dz], over_send.at[dz], over_recv.at[dz], across
                )
                copy.start()
                crossing[dz] = copy
                pending.append(copy)

        def share(dz):
            part = src[chip_of(dz, 0)].astype(F32)
            if ny > 1:
                crossing[dz].wait_recv()
                part = part + over[dz].astype(F32)
            return part

        copies = []
        for dz in range(1, nz):
            mid[dz] = share(dz).astype(BF16)
            copy = remote(
                mid.at[dz], dst.at[dz], send.at[dz], recv.at[dz], chip_of(dz, 0) * CORES + k
            )
            copy.start()
            copies.append(copy)
            pending.append(copy)
        total = share(0)
        for dz in range(1, nz):
            copies[dz - 1].wait_recv()
            total = total + dst[dz].astype(F32)
        return total

    after = (res_ref[...].astype(F32) + send_home(ost, y2, mid2, r2, yb_send, yb_recv, b_send, b_recv)).astype(BF16)
    aft[...] = after
    middle = after.astype(F32)
    inv = lax.rsqrt(jnp.mean(middle * middle, axis=-1, keepdims=True) + 1e-06)
    xn[k, c] = (middle * inv * gain_ref[...].astype(F32).reshape(1, model)).astype(BF16)
    gather(xn, x_sems)

    for copy in ld_w:
        copy.wait()
    ff = wg.shape[2]
    ftile = 256
    lane = lax.broadcasted_iota(jnp.int32, (all_rows, 128), 1)
    experts = wg.shape[0]
    for e in range(experts):

        def enter(i, carry):
            cols = pl.ds(pl.multiple_of(i * ftile, 128), ftile)
            x = xn[...].reshape(all_rows, model)
            gate = jnp.dot(x, wg[e, :, cols], preferred_element_type=F32)
            up = jnp.dot(x, wu[e, :, cols], preferred_element_type=F32)
            hid[:, cols] = (gate / (1.0 + jnp.exp(-gate)) * up).astype(BF16)
            return carry

        lax.fori_loop(0, ff // ftile, enter, 0)
        table = coef[...].reshape(all_rows, 128)
        share = jnp.sum(jnp.where(lane == me * experts + e, table, 0.0), axis=1, keepdims=True)

        def leave(i, carry):
            cols = pl.ds(pl.multiple_of(i * tile, 128), tile)
            made = jnp.dot(hid[...], wd[e, :, cols], preferred_element_type=F32)
            made = share * made.astype(BF16).astype(F32)
            if e == 0:
                acc[:, cols] = made
            else:
                acc[:, cols] += made
            return carry

        lax.fori_loop(0, model // tile, leave, 0)

    own_part = pl.ds(pl.multiple_of(k * half_rows, 128), half_rows)
    other_part = pl.ds(pl.multiple_of((1 - k) * half_rows, 128), half_rows)
    es[...] = acc[other_part, :].astype(BF16)
    swap = remote(es, er, e_sems.at[0], e_sems.at[1], sister)
    swap.start()
    pending.append(swap)
    swap.wait_recv()
    ost3[...] = (acc[own_part, :] + er[...].astype(F32)).astype(BF16).reshape(chips, rows, model)
    mixed = send_home(ost3, y3, mid3, r3, yd_send, yd_recv, d_send, d_recv)
    out_ref[...] = (aft[...].astype(F32) + mixed).astype(BF16)

    for copy in pending:
        copy.wait_send()

    def drain(jc, carry):
        if ny > 1:

            @pl.when(jnp.logical_not(is_mine(jc)))
            def _():
                for copy in part_cross(jc):
                    copy.wait_send()

        for dz, dk in lines:
            q_line(jc, dz, dk).wait_send()
        for dy in range(1, ny):
            for dz, dk in [(0, 0)] + lines:
                q_cross(jc, dz, dk, dy).wait_send()
        for dk in range(CORES):
            is_far, far, near = part_copies(jc, dk)

            @pl.when(jnp.logical_and(is_far, is_mine(jc)))
            def _():
                for copy in far:
                    copy.wait_send()

        return carry

    lax.fori_loop(0, half_chips, drain, 0)


def on_device(
    ny,
    queries,
    new_key,
    new_value,
    key_cache,
    value_cache,
    cache_len,
    out_weight,
    residual,
    norm_gain,
    expert_ids,
    route_weight,
    w_gate,
    w_up,
    w_down,
):
    n = lax.axis_size("ctx")
    chips = n // CORES
    nz = chips // ny
    hpc = HEADS // chips
    rows = queries.shape[0]
    model = residual.shape[1]
    here = key_cache.shape[0]
    ff = w_gate.shape[2]
    all_rows, half_rows = n * rows, chips * rows
    half_chips = chips // CORES
    pairs = half_chips // ny
    kv_width = key_cache.shape[1] // CORES
    lens = jnp.transpose(cache_len.reshape(chips, CORES, rows), (1, 0, 2)).reshape(1, all_rows)
    stat_rows = max(8, 2 * hpc)
    any_space = pl.BlockSpec(memory_space=pl.ANY)
    vmem = pl.BlockSpec(memory_space=pltpu.VMEM)
    dma = lambda *dims: pltpu.SemaphoreType.DMA(dims)
    gather_sems = [dma(nz), dma(nz), dma(ny * nz), dma(ny * nz), dma(ny * nz), dma(ny * nz)]
    return pl.pallas_call(
        functools.partial(layer_kernel, n, ny),
        out_shape=jax.ShapeDtypeStruct((rows, model), BF16),
        in_specs=[vmem] * 5 + [any_space] * 2 + [vmem, any_space, vmem, vmem] + [any_space] * 3,
        out_specs=vmem,
        scratch_shapes=[
            pltpu.VMEM((half_chips, CORES, chips, rows, hpc * HD), BF16),
            pltpu.VMEM((CORES, here, kv_width), BF16),
            pltpu.VMEM((CORES, here, kv_width), BF16),
            pltpu.VMEM((kv_width // HD, HD + 16, CORES * here), BF16),
            pltpu.VMEM((CORES, chips, rows, 128), F32),
            pltpu.VMEM((chips, rows, HD), BF16),
            pltpu.VMEM((chips, rows, HD), F32),
            pltpu.VMEM((chips, rows, HD), F32),
            pltpu.VMEM((CORES * here, all_rows), F32),
            pltpu.VMEM((chips // CORES, CORES, hpc * HD, half_rows), BF16),
            pltpu.VMEM((chips // CORES, CORES, stat_rows, half_rows), F32),
            pltpu.VMEM((pairs, CORES, hpc * HD, half_rows), BF16),
            pltpu.VMEM((pairs, CORES, stat_rows, half_rows), F32),
            pltpu.VMEM((pairs, CORES, hpc * HD, half_rows), BF16),
            pltpu.VMEM((pairs, CORES, stat_rows, half_rows), F32),
            pltpu.VMEM((nz, hpc * HD, half_rows), BF16),
            pltpu.VMEM((nz, stat_rows, half_rows), F32),
            pltpu.VMEM((CORES,) + out_weight.shape, BF16),
            pltpu.VMEM((half_rows, hpc * HD), BF16),
            pltpu.VMEM((chips, rows, model), BF16),
            pltpu.VMEM((nz, rows, model), BF16),
            pltpu.VMEM((nz, rows, model), BF16),
            pltpu.VMEM((nz, rows, model), BF16),
            pltpu.VMEM((CORES, chips, rows, model), BF16),
            pltpu.VMEM(w_gate.shape, BF16),
            pltpu.VMEM(w_up.shape, BF16),
            pltpu.VMEM(w_down.shape, BF16),
            pltpu.VMEM((all_rows, ff), BF16),
            pltpu.VMEM((all_rows, model), F32),
            pltpu.VMEM((half_rows, model), BF16),
            pltpu.VMEM((half_rows, model), BF16),
            pltpu.VMEM((chips, rows, model), BF16),
            pltpu.VMEM((nz, rows, model), BF16),
            pltpu.VMEM((nz, rows, model), BF16),
            pltpu.VMEM((nz, rows, model), BF16),
            pltpu.VMEM((rows, model), BF16),
            dma(half_chips + 8),
            dma(3),
            dma(3),
            dma(half_chips, nz * CORES),
            dma(half_chips, nz * CORES),
            dma(half_chips, ny * nz * CORES),
            dma(half_chips, ny * nz * CORES),
            gather_sems,
            dma(2, chips),
            dma(2, chips),
            dma(2, pairs),
            dma(2, pairs),
            dma(2, chips),
            dma(2, chips),
            dma(nz),
            dma(nz),
            dma(nz),
            dma(nz),
            gather_sems,
            dma(2),
            dma(nz),
            dma(nz),
            dma(nz),
            dma(nz),
        ],
        compiler_params=pltpu.CompilerParams(
            collective_id=0, has_side_effects=True, vmem_limit_bytes=60 * 1024 * 1024
        ),
    )(
        queries,
        new_key,
        new_value,
        expert_ids,
        route_weight,
        key_cache,
        value_cache,
        lens,
        out_weight,
        residual,
        norm_gain,
        w_gate,
        w_up,
        w_down,
    )


def solution(mesh):
    rowed = P(("groups", "ctx"), None)
    placed = (
        rowed,
        rowed,
        rowed,
        rowed,
        rowed,
        P("groups"),
        P("ctx", None),
        rowed,
        P(),
        rowed,
        rowed,
        P("ctx", None, None),
        P("ctx", None, None),
        P("ctx", None, None),
    )
    ny = 2 if mesh.shape["groups"] == 2 else 1
    return jax.shard_map(
        functools.partial(on_device, ny),
        mesh=mesh,
        in_specs=placed,
        out_specs=rowed,
        check_vma=False,
    )
```

```python
import functools
import math

import jax
import jax.numpy as jnp
from jax import lax
from jax.experimental import pallas as pl
from jax.experimental.pallas import tpu as pltpu
from jax.sharding import PartitionSpec as P

HEADS = 32
KVH = 4
HD = 128
GROUP = HEADS // KVH
CORES = 2
NEG = -1e30
FLOOR = -1e29
MESH = pl.DeviceIdType.MESH
F32 = jnp.float32
BF16 = jnp.bfloat16
SCALE2 = math.log2(math.e) / math.sqrt(HD)


def remote(src, dst, send, recv, target):
    return pltpu.make_async_remote_copy(
        src_ref=src,
        dst_ref=dst,
        send_sem=send,
        recv_sem=recv,
        device_id={"ctx": target},
        device_id_type=MESH,
    )


def layer_kernel(
    n,
    ny,
    q_in,
    nk_ref,
    nv_in,
    ids_ref,
    share_ref,
    kc_in,
    vc_in,
    len_ref,
    ow_in,
    res_ref,
    gain_ref,
    wg_in,
    wu_in,
    wd_in,
    out_ref,
    q_all,
    kc,
    vc,
    vt,
    coef,
    nvr,
    fs,
    fsr,
    bias,
    num,
    stat,
    ynum,
    ystat,
    mnum,
    mstat,
    rnum,
    rstat,
    ow,
    att,
    ost,
    y2,
    mid2,
    r2,
    xn,
    wg,
    wu,
    wd,
    hid,
    acc,
    es,
    er,
    ost3,
    y3,
    mid3,
    r3,
    aft,
    load_sem,
    kv_send,
    kv_recv,
    q_send,
    q_recv,
    q_relay_send,
    q_relay_recv,
    c_sems,
    f_send,
    f_recv,
    ya_send,
    ya_recv,
    a_send,
    a_recv,
    yb_send,
    yb_recv,
    b_send,
    b_recv,
    x_sems,
    e_sems,
    yd_send,
    yd_recv,
    d_send,
    d_recv,
):
    chips = n // CORES
    nz = chips // ny
    half_chips = chips // CORES
    hpc = HEADS // chips
    rows = q_in.shape[0]
    all_rows = n * rows
    half_rows = chips * rows
    width = q_in.shape[1] // CORES
    kv_width = kc_in.shape[1] // CORES
    here = kc_in.shape[0]
    model = res_ref.shape[1]
    me = lax.axis_index("ctx")
    k = lax.rem(me, CORES)
    c = me // CORES
    z = c // ny
    y = lax.rem(c, ny)
    sister = c * CORES + 1 - k

    def chip_of(dz, dy):
        return lax.rem(z + dz, nz) * ny + lax.rem(y + dy, ny)

    loads = []

    def load(src, dst):
        copy = pltpu.make_async_copy(src, dst, load_sem.at[len(loads)])
        copy.start()
        loads.append(copy)
        return copy

    own_cols = pl.ds(pl.multiple_of(k * kv_width, 128), kv_width)
    other_cols = pl.ds(pl.multiple_of((1 - k) * kv_width, 128), kv_width)
    ld_k = load(kc_in.at[:, own_cols], kc.at[k])
    ld_v = load(vc_in.at[:, own_cols], vc.at[k])
    chunk = hpc * HD

    across = chip_of(0, 1) * CORES + k

    def order_at(line, jc):
        return lax.rem(line + 1 + jc // ny, half_chips // ny) * ny + lax.rem(jc, ny)

    def q_cols(core, order):
        return pl.ds(pl.multiple_of(core * width + order * chunk, 128), chunk)

    ld_q = [
        load(q_in.at[:, q_cols(k, order)], q_all.at[order, k, c]) for order in range(half_chips)
    ]
    kv_head = (c * hpc) // GROUP
    ld_nv = load(
        nv_in.at[:, pl.ds(pl.multiple_of(kv_head * HD, 128), HD)], nvr.at[c]
    )
    ld_ow = load(ow_in, ow.at[k])

    barrier = pltpu.get_barrier_semaphore()
    for i in range(1, n):
        pl.semaphore_signal(
            barrier, inc=1, device_id={"ctx": lax.rem(me + i, n)}, device_id_type=MESH
        )
    pl.semaphore_wait(barrier, n - 1)

    pending = []

    kv_copies = []
    for i, (src, dst) in enumerate(
        ((kc_in.at[:, other_cols], kc.at[k]), (vc_in.at[:, other_cols], vc.at[k]), (ow_in, ow.at[k]))
    ):
        copy = remote(src, dst, kv_send.at[i], kv_recv.at[i], sister)
        copy.start()
        kv_copies.append(copy)
        pending.append(copy)

    lines = [(dz, dk) for dz in range(nz) for dk in range(CORES) if (dz, dk) != (0, 0)]

    def q_line(jc, dz, dk):
        kt = lax.rem(k + dk, CORES)
        order = order_at(lax.rem(z + dz, nz), jc)
        slot = dz * CORES + dk
        return remote(
            q_in.at[:, q_cols(kt, order)],
            q_all.at[order, k, c],
            q_send.at[jc, slot],
            q_recv.at[jc, slot],
            chip_of(dz, 0) * CORES + kt,
        )

    def q_cross(jc, dz, dk, dy):
        order = order_at(z, jc)
        core, chip = lax.rem(k + dk, CORES), chip_of(nz - dz, 0)
        held = q_all.at[order, core, chip]
        src = q_in.at[:, q_cols(k, order)] if (dz, dk) == (0, 0) else held
        slot = ((dy - 1) * nz + dz) * CORES + dk
        return remote(
            src,
            held,
            q_relay_send.at[jc, slot],
            q_relay_recv.at[jc, slot],
            chip_of(0, dy) * CORES + k,
        )

    def q_send_all(jc):
        for dy in range(1, ny):
            q_cross(jc, 0, 0, dy).start()
        for dz, dk in lines:
            q_line(jc, dz, dk).start()

    def q_relay(jc):
        for dz, dk in lines:
            q_line(jc, dz, dk).wait_recv()
            for dy in range(1, ny):
                q_cross(jc, dz, dk, dy).start()

    def q_arrive(jc):
        for dy in range(1, ny):
            for dz, dk in [(0, 0)] + lines:
                q_cross(jc, dz, dk, dy).wait_recv()

    for jc in range(half_chips):
        q_send_all(jc)

    lane = lax.broadcasted_iota(jnp.int32, (rows, 128), 1)
    for chip in range(chips):
        tile = jnp.zeros((rows, 128), F32)
        for hh in range(hpc):
            h = chip * hpc + hh
            g = h // GROUP
            qv = q_in[:, h * HD : (h + 1) * HD].astype(F32)
            kv = nk_ref[:, g * HD : (g + 1) * HD].astype(F32)
            score = jnp.sum(qv * kv, axis=1, keepdims=True) * SCALE2
            tile = jnp.where(lane == hh, score, tile)
        fs[chip] = tile
    table = jnp.zeros((rows, 128), F32)
    for t in range(ids_ref.shape[1]):
        table = table + jnp.where(lane == ids_ref[:, t : t + 1], share_ref[:, t : t + 1], 0.0)
    coef[k, c] = table
    fsr[c] = fs[c]

    fresh_copies = []
    for j in range(1, chips):
        target = lax.rem(c + j, chips)
        cols = pl.ds(pl.multiple_of(((target * hpc) // GROUP) * HD, 128), HD)
        for i, (src, dst) in enumerate(((nv_in.at[:, cols], nvr.at[c]), (fs.at[target], fsr.at[c]))):
            copy = remote(src, dst, f_send.at[i, j], f_recv.at[i, j], target * CORES + k)
            copy.start()
            fresh_copies.append(copy)
            pending.append(copy)

    for src, dst in ((wg_in, wg), (wu_in, wu), (wd_in, wd)):
        load(src, dst)
    ld_w = loads[-3:]

    def gather(buf, sems):
        z_send, z_recv, y_send, y_recv, s_send, s_recv = sems
        along = []
        for dz in range(1, nz):
            copy = remote(
                buf.at[k, c], buf.at[k, c], z_send.at[dz], z_recv.at[dz], chip_of(dz, 0) * CORES + k
            )
            copy.start()
            along.append(copy)
            pending.append(copy)
        crossed, shared = [], []

        def cross(dz):
            source = chip_of(nz - dz, 0)
            for dy in range(1, ny):
                slot = dy * nz + dz
                copy = remote(
                    buf.at[k, source],
                    buf.at[k, source],
                    y_send.at[slot],
                    y_recv.at[slot],
                    chip_of(0, dy) * CORES + k,
                )
                copy.start()
                crossed.append((dz, dy, copy))
                pending.append(copy)

        def share(dz, dy):
            source = chip_of(nz - dz, ny - dy)
            slot = dy * nz + dz
            copy = remote(
                buf.at[k, source], buf.at[k, source], s_send.at[slot], s_recv.at[slot], sister
            )
            copy.start()
            shared.append(copy)
            pending.append(copy)

        cross(0)
        share(0, 0)
        for dz in range(1, nz):
            along[dz - 1].wait_recv()
            cross(dz)
            share(dz, 0)
        for dz, dy, copy in crossed:
            copy.wait_recv()
            share(dz, dy)
        for copy in shared:
            copy.wait_recv()

    q_relay(0)
    ld_k.wait()
    ld_v.wait()
    for copy in ld_q:
        copy.wait()
    kv_copies[0].wait_recv()
    kv_copies[1].wait_recv()
    kv_heads = kv_width // HD
    for g in range(kv_heads):
        vt[g, :HD] = jnp.transpose(vc[:, :, g * HD : (g + 1) * HD].reshape(CORES * here, HD))
        vt[g, HD:] = jnp.ones((vt.shape[1] - HD, CORES * here), BF16)

    stat[...] = jnp.zeros_like(stat)
    seen = len_ref[...] - c * (CORES * here)
    place = lax.broadcasted_iota(jnp.int32, bias.shape, 0)
    bias[...] = jnp.where(place < seen, 0.0, NEG)
    q_relay(1)
    stat_half = stat.shape[2] // 2

    def part_copies(jc, dk):
        order = order_at(z, jc)
        owner = k * half_chips + order
        kt = lax.rem(k + dk, CORES)
        slot = jc * CORES + dk
        if ny > 1:
            held = (mnum.at[order // ny, kt], mstat.at[order // ny, kt])
        else:
            held = (num.at[order, kt], stat.at[order, kt])
        pairs = tuple(zip(held, (rnum.at[z], rstat.at[z])))
        far = [
            remote(src, dst, a_send.at[i, slot], a_recv.at[i, z], owner * CORES + kt)
            for i, (src, dst) in enumerate(pairs)
        ]
        near = [
            pltpu.make_async_copy(src, dst, a_recv.at[i, z]) for i, (src, dst) in enumerate(pairs)
        ]
        return owner * CORES + kt != me, far, near

    def part_start(jc):
        for dk in range(CORES):
            is_far, far, near = part_copies(jc, dk)

            @pl.when(is_far)
            def _():
                for copy in far:
                    copy.start()

            @pl.when(jnp.logical_not(is_far))
            def _():
                for copy in near:
                    copy.start()

    def part_cross(jc):
        order = order_at(z, jc)
        pair = order // ny
        return [
            remote(src.at[order], dst.at[pair], ya_send.at[i, pair], ya_recv.at[i, pair], across)
            for i, (src, dst) in enumerate(((num, ynum), (stat, ystat)))
        ]

    def is_mine(jc):
        return lax.rem(order_at(z, jc), ny) == y

    def part_merge(jc):
        order = order_at(z, jc)
        pair = order // ny
        for copy in part_cross(jc):
            copy.wait_recv()
        for kt in range(CORES):
            for hh in range(hpc):
                cut = slice(hh * HD, (hh + 1) * HD)
                m1, l1 = (stat[order, kt, r : r + 1, :] for r in (hh, stat_half + hh))
                m2, l2 = (ystat[pair, kt, r : r + 1, :] for r in (hh, stat_half + hh))
                m = jnp.maximum(m1, m2)
                w1, w2 = jnp.exp2(m1 - m), jnp.exp2(m2 - m)
                mnum[pair, kt, cut, :] = (
                    w1 * num[order, kt, cut, :].astype(F32)
                    + w2 * ynum[pair, kt, cut, :].astype(F32)
                ).astype(BF16)
                mstat[pair, kt, hh : hh + 1, :] = m
                mstat[pair, kt, stat_half + hh : stat_half + hh + 1, :] = w1 * l1 + w2 * l2
        part_start(jc)

    def owner_step(jc, carry):
        order = order_at(z, jc)

        q_arrive(jc)

        def scores(hh):
            g = (order * hpc + hh) // GROUP
            at = pl.ds(pl.multiple_of(hh * HD, HD), HD)
            qh = q_all[order, :, :, :, at].reshape(all_rows, HD)
            kh = kc[:, :, pl.ds(pl.multiple_of(g * HD, 128), HD)].reshape(CORES * here, HD)
            s = lax.dot_general(kh, qh, (((1,), (1,)), ((), ())), preferred_element_type=F32)
            return g, s * SCALE2 + bias[...]

        def finish(hh, g, t):
            m = jnp.maximum(jnp.max(t, axis=0, keepdims=True), FLOOR)
            p = jnp.exp2(t - m).astype(BF16)
            o = jnp.dot(vt[g], p, preferred_element_type=F32)
            total = o[HD : HD + 1, :]
            o = o[:HD, :].astype(BF16)
            at = pl.ds(pl.multiple_of(hh * HD, HD), HD)
            for kt in range(CORES):
                cut = slice(kt * half_rows, (kt + 1) * half_rows)
                num[order, kt, at, :] = o[:, cut]
                stat[order, kt, pl.ds(hh, 1), :] = m[:, cut]
                stat[order, kt, pl.ds(stat_half + hh, 1), :] = total[:, cut]

        pairs = hpc // 2

        def head_step(i, carry):
            @pl.when(jnp.logical_and(i == pairs // 2, jc + 2 < half_chips))
            def _():
                q_relay(jc + 2)

            both = [(2 * i + u, *scores(2 * i + u)) for u in range(2)]
            for hh, g, t in both:
                finish(hh, g, t)
            return carry

        lax.fori_loop(0, pairs, head_step, 0)
        if ny == 1:
            part_start(jc)
            return carry

        @pl.when(jnp.logical_not(is_mine(jc)))
        def _():
            for copy in part_cross(jc):
                copy.start()

        before = jnp.maximum(jc - 1, 0)

        @pl.when(jnp.logical_and(jc > 0, is_mine(before)))
        def _():
            part_merge(before)

        return carry

    lax.fori_loop(0, half_chips, owner_step, 0)
    if ny > 1:

        @pl.when(is_mine(half_chips - 1))
        def _():
            part_merge(half_chips - 1)

    gather(coef, c_sems)
    ld_nv.wait()
    ld_ow.wait()
    kv_copies[2].wait_recv()
    for copy in fresh_copies:
        copy.wait_recv()
    for i in range(nz):
        pltpu.make_async_copy(rnum.at[i], rnum.at[i], a_recv.at[0, i]).wait()
        pltpu.make_async_copy(rstat.at[i], rstat.at[i], a_recv.at[1, i]).wait()

    fresh_t = jnp.transpose(fsr[...].reshape(half_rows, HD))
    value_t = jnp.transpose(nvr[...].astype(F32).reshape(half_rows, HD))
    for hh in range(hpc):
        fresh = fresh_t[hh : hh + 1, :]
        peak = fresh
        for i in range(nz):
            peak = jnp.maximum(peak, rstat[i, hh : hh + 1, :])
        w = jnp.exp2(fresh - peak)
        den = w
        top = w * value_t
        for i in range(nz):
            w = jnp.exp2(rstat[i, hh : hh + 1, :] - peak)
            den = den + w * rstat[i, stat_half + hh : stat_half + hh + 1, :]
            top = top + w * rnum[i, hh * HD : (hh + 1) * HD, :].astype(F32)
        att[:, hh * HD : (hh + 1) * HD] = jnp.transpose(top / den).astype(BF16)

    tile = 512

    def project(i, carry):
        cols = pl.ds(pl.multiple_of(i * tile, 128), tile)
        weight = ow[:, :, cols].reshape(hpc * HD, tile)
        part = jnp.dot(att[...], weight, preferred_element_type=F32).astype(BF16)
        ost[:, :, cols] = part.reshape(chips, rows, tile)
        return carry

    lax.fori_loop(0, model // tile, project, 0)

    def send_home(src, over, mid, dst, over_send, over_recv, send, recv):
        crossing = {}
        if ny > 1:
            for dz in [*range(1, nz), 0]:
                copy = remote(
                    src.at[chip_of(dz, 1)], over.at[dz], over_send.at[dz], over_recv.at[dz], across
                )
                copy.start()
                crossing[dz] = copy
                pending.append(copy)

        def share(dz):
            part = src[chip_of(dz, 0)].astype(F32)
            if ny > 1:
                crossing[dz].wait_recv()
                part = part + over[dz].astype(F32)
            return part

        copies = []
        for dz in range(1, nz):
            mid[dz] = share(dz).astype(BF16)
            copy = remote(
                mid.at[dz], dst.at[dz], send.at[dz], recv.at[dz], chip_of(dz, 0) * CORES + k
            )
            copy.start()
            copies.append(copy)
            pending.append(copy)
        total = share(0)
        for dz in range(1, nz):
            copies[dz - 1].wait_recv()
            total = total + dst[dz].astype(F32)
        return total

    after = (res_ref[...].astype(F32) + send_home(ost, y2, mid2, r2, yb_send, yb_recv, b_send, b_recv)).astype(BF16)
    aft[...] = after
    middle = after.astype(F32)
    inv = lax.rsqrt(jnp.mean(middle * middle, axis=-1, keepdims=True) + 1e-06)
    xn[k, c] = (middle * inv * gain_ref[...].astype(F32).reshape(1, model)).astype(BF16)
    gather(xn, x_sems)

    for copy in ld_w:
        copy.wait()
    ff = wg.shape[2]
    ftile = 256
    lane = lax.broadcasted_iota(jnp.int32, (all_rows, 128), 1)
    experts = wg.shape[0]
    for e in range(experts):

        def enter(i, carry):
            cols = pl.ds(pl.multiple_of(i * ftile, 128), ftile)
            x = xn[...].reshape(all_rows, model)
            gate = jnp.dot(x, wg[e, :, cols], preferred_element_type=F32)
            up = jnp.dot(x, wu[e, :, cols], preferred_element_type=F32)
            hid[:, cols] = (gate / (1.0 + jnp.exp(-gate)) * up).astype(BF16)
            return carry

        lax.fori_loop(0, ff // ftile, enter, 0)
        table = coef[...].reshape(all_rows, 128)
        share = jnp.sum(jnp.where(lane == me * experts + e, table, 0.0), axis=1, keepdims=True)

        def leave(i, carry):
            cols = pl.ds(pl.multiple_of(i * tile, 128), tile)
            made = jnp.dot(hid[...], wd[e, :, cols], preferred_element_type=F32)
            made = share * made.astype(BF16).astype(F32)
            if e == 0:
                acc[:, cols] = made
            else:
                acc[:, cols] += made
            return carry

        lax.fori_loop(0, model // tile, leave, 0)

    own_part = pl.ds(pl.multiple_of(k * half_rows, 128), half_rows)
    other_part = pl.ds(pl.multiple_of((1 - k) * half_rows, 128), half_rows)
    es[...] = acc[other_part, :].astype(BF16)
    swap = remote(es, er, e_sems.at[0], e_sems.at[1], sister)
    swap.start()
    pending.append(swap)
    swap.wait_recv()
    ost3[...] = (acc[own_part, :] + er[...].astype(F32)).astype(BF16).reshape(chips, rows, model)
    mixed = send_home(ost3, y3, mid3, r3, yd_send, yd_recv, d_send, d_recv)
    out_ref[...] = (aft[...].astype(F32) + mixed).astype(BF16)

    for copy in pending:
        copy.wait_send()

    def drain(jc, carry):
        if ny > 1:

            @pl.when(jnp.logical_not(is_mine(jc)))
            def _():
                for copy in part_cross(jc):
                    copy.wait_send()

        for dz, dk in lines:
            q_line(jc, dz, dk).wait_send()
        for dy in range(1, ny):
            for dz, dk in [(0, 0)] + lines:
                q_cross(jc, dz, dk, dy).wait_send()
        for dk in range(CORES):
            is_far, far, near = part_copies(jc, dk)

            @pl.when(jnp.logical_and(is_far, is_mine(jc)))
            def _():
                for copy in far:
                    copy.wait_send()

        return carry

    lax.fori_loop(0, half_chips, drain, 0)


def on_device(
    ny,
    queries,
    new_key,
    new_value,
    key_cache,
    value_cache,
    cache_len,
    out_weight,
    residual,
    norm_gain,
    expert_ids,
    route_weight,
    w_gate,
    w_up,
    w_down,
):
    n = lax.axis_size("ctx")
    chips = n // CORES
    nz = chips // ny
    hpc = HEADS // chips
    rows = queries.shape[0]
    model = residual.shape[1]
    here = key_cache.shape[0]
    ff = w_gate.shape[2]
    all_rows, half_rows = n * rows, chips * rows
    half_chips = chips // CORES
    pairs = half_chips // ny
    kv_width = key_cache.shape[1] // CORES
    lens = jnp.transpose(cache_len.reshape(chips, CORES, rows), (1, 0, 2)).reshape(1, all_rows)
    stat_rows = max(8, 2 * hpc)
    any_space = pl.BlockSpec(memory_space=pl.ANY)
    vmem = pl.BlockSpec(memory_space=pltpu.VMEM)
    dma = lambda *dims: pltpu.SemaphoreType.DMA(dims)
    gather_sems = [dma(nz), dma(nz), dma(ny * nz), dma(ny * nz), dma(ny * nz), dma(ny * nz)]
    return pl.pallas_call(
        functools.partial(layer_kernel, n, ny),
        out_shape=jax.ShapeDtypeStruct((rows, model), BF16),
        in_specs=[vmem] * 5 + [any_space] * 2 + [vmem, any_space, vmem, vmem] + [any_space] * 3,
        out_specs=vmem,
        scratch_shapes=[
            pltpu.VMEM((half_chips, CORES, chips, rows, hpc * HD), BF16),
            pltpu.VMEM((CORES, here, kv_width), BF16),
            pltpu.VMEM((CORES, here, kv_width), BF16),
            pltpu.VMEM((kv_width // HD, HD + 16, CORES * here), BF16),
            pltpu.VMEM((CORES, chips, rows, 128), F32),
            pltpu.VMEM((chips, rows, HD), BF16),
            pltpu.VMEM((chips, rows, HD), F32),
            pltpu.VMEM((chips, rows, HD), F32),
            pltpu.VMEM((CORES * here, all_rows), F32),
            pltpu.VMEM((chips // CORES, CORES, hpc * HD, half_rows), BF16),
            pltpu.VMEM((chips // CORES, CORES, stat_rows, half_rows), F32),
            pltpu.VMEM((pairs, CORES, hpc * HD, half_rows), BF16),
            pltpu.VMEM((pairs, CORES, stat_rows, half_rows), F32),
            pltpu.VMEM((pairs, CORES, hpc * HD, half_rows), BF16),
            pltpu.VMEM((pairs, CORES, stat_rows, half_rows), F32),
            pltpu.VMEM((nz, hpc * HD, half_rows), BF16),
            pltpu.VMEM((nz, stat_rows, half_rows), F32),
            pltpu.VMEM((CORES,) + out_weight.shape, BF16),
            pltpu.VMEM((half_rows, hpc * HD), BF16),
            pltpu.VMEM((chips, rows, model), BF16),
            pltpu.VMEM((nz, rows, model), BF16),
            pltpu.VMEM((nz, rows, model), BF16),
            pltpu.VMEM((nz, rows, model), BF16),
            pltpu.VMEM((CORES, chips, rows, model), BF16),
            pltpu.VMEM(w_gate.shape, BF16),
            pltpu.VMEM(w_up.shape, BF16),
            pltpu.VMEM(w_down.shape, BF16),
            pltpu.VMEM((all_rows, ff), BF16),
            pltpu.VMEM((all_rows, model), F32),
            pltpu.VMEM((half_rows, model), BF16),
            pltpu.VMEM((half_rows, model), BF16),
            pltpu.VMEM((chips, rows, model), BF16),
            pltpu.VMEM((nz, rows, model), BF16),
            pltpu.VMEM((nz, rows, model), BF16),
            pltpu.VMEM((nz, rows, model), BF16),
            pltpu.VMEM((rows, model), BF16),
            dma(half_chips + 8),
            dma(3),
            dma(3),
            dma(half_chips, nz * CORES),
            dma(half_chips, nz * CORES),
            dma(half_chips, ny * nz * CORES),
            dma(half_chips, ny * nz * CORES),
            gather_sems,
            dma(2, chips),
            dma(2, chips),
            dma(2, pairs),
            dma(2, pairs),
            dma(2, chips),
            dma(2, chips),
            dma(nz),
            dma(nz),
            dma(nz),
            dma(nz),
            gather_sems,
            dma(2),
            dma(nz),
            dma(nz),
            dma(nz),
            dma(nz),
        ],
        compiler_params=pltpu.CompilerParams(
            collective_id=0, has_side_effects=True, vmem_limit_bytes=60 * 1024 * 1024
        ),
    )(
        queries,
        new_key,
        new_value,
        expert_ids,
        route_weight,
        key_cache,
        value_cache,
        lens,
        out_weight,
        residual,
        norm_gain,
        w_gate,
        w_up,
        w_down,
    )


def solution(mesh):
    rowed = P(("groups", "ctx"), None)
    placed = (
        rowed,
        rowed,
        rowed,
        rowed,
        rowed,
        P("groups"),
        P("ctx", None),
        rowed,
        P(),
        rowed,
        rowed,
        P("ctx", None, None),
        P("ctx", None, None),
        P("ctx", None, None),
    )
    ny = 2 if mesh.shape["groups"] == 2 else 1
    return jax.shard_map(
        functools.partial(on_device, ny),
        mesh=mesh,
        in_specs=placed,
        out_specs=rowed,
        check_vma=False,
    )
```
